32 devices in a mesh: row: 8 (over y, x, core), col: 4 (over z).
Axes of the slice: x: 2, y: 2, z: 4, core: 2. Of those that a mesh axis runs over, the one named last changes fastest.
Arguments:
- panel: int32 [32], replicated, may hold values from 0 to 31, each once
- trailing: float32 [8192, 8192], P('row', 'col'), as said below
Outputs:
- factor_panels: float32 [8192, 768], P('row')
- schur: float32 [8192, 8192], P('row', 'col')
The draws below stay inside these ranges and needn't reach their ends.
Inputs may be any that keep to these rules, and one draw needn't show every extreme that they name: panel names every block index once. In matrix order trailing is symmetric, and each diagonal block of 256 x 256 is strictly diagonally dominant with a positive diagonal.
All inputs are finite; a program needn't handle non-finite values.
Results may differ from the reference program's by a relative error of at most 0.0001.
Values sent between devices are 32-bit elements; how exact they have to be, the bound alone decides.
No kernel may reach another device: no remote copies, remote signals or barrier semaphores. Data moves between devices by JAX's collectives and lax.ppermute only.
A program may use at most 128 MiB of HBM per device.

```python
import math
import jax
import jax.numpy as jnp
from jax import lax

NB = 256
BLK = 4
PANELS = 3
GRID = 32
ORDER = 8192
N_ROW = 8
N_COL = 4


def draw_trailing(key, part):
    first, second = jax.random.split(key, 2)
    raw = jax.random.uniform(first, (ORDER, ORDER), jnp.float32, -1.0, 1.0)
    sym = (raw + raw.T) * 0.5
    blocks = jnp.arange(ORDER) // NB
    same = blocks[:, None] == blocks[None, :]
    sym = jnp.where(same, 0.3 * sym, sym)
    base = 0.3 * NB + 4.0
    diagonal = base * jnp.exp(jax.random.uniform(second, (ORDER,), jnp.float32) * math.log(2.0))
    places = jnp.arange(ORDER)
    full = jnp.where(places[:, None] == places[None, :], diagonal[:, None], sym)
    block_cols = GRID // N_COL
    full = full.reshape(BLK, N_ROW, NB, ORDER).transpose(1, 0, 2, 3).reshape(ORDER, ORDER)
    full = full.reshape(ORDER, block_cols, N_COL, NB).transpose(0, 2, 1, 3).reshape(ORDER, ORDER)
    return full.astype(jnp.float32)


def setup_inputs(seed: int = 0) -> dict:
    arg_keys = jax.random.split(jax.random.key(seed), 3)
    return {
        "panel": jax.random.permutation(arg_keys[0], GRID).astype(jnp.int32),
        "trailing": draw_trailing(jax.random.fold_in(arg_keys[2], 71), 0),
    }


def to_matrix(slots):
    block_cols = GRID // N_COL
    ordered = slots.reshape(N_ROW, BLK, NB, ORDER).transpose(1, 0, 2, 3).reshape(ORDER, ORDER)
    return ordered.reshape(ORDER, N_COL, block_cols, NB).transpose(0, 2, 1, 3).reshape(ORDER, ORDER)

def rows_to_slots(matrix):
    width = matrix.shape[1]
    return matrix.reshape(BLK, N_ROW, NB, width).transpose(1, 0, 2, 3).reshape(ORDER, width)

def cols_to_slots(matrix):
    block_cols = GRID // N_COL
    return matrix.reshape(ORDER, block_cols, N_COL, NB).transpose(0, 2, 1, 3).reshape(ORDER, ORDER)

def reference(panel, trailing):
    current = to_matrix(trailing)
    indices = jnp.arange(ORDER, dtype=jnp.int32) // NB
    factors = []
    for step in range(PANELS):
        pivot = panel[step].astype(jnp.int32)
        columns = lax.dynamic_slice_in_dim(current, pivot * NB, NB, 1)
        corner = lax.dynamic_slice_in_dim(columns, pivot * NB, NB, 0)
        lower = jnp.linalg.cholesky(corner)
        factor = lax.linalg.triangular_solve(lower, columns.T, left_side=True, lower=True).T
        current = current - jnp.dot(factor.astype(jnp.float32), factor.T.astype(jnp.float32), precision=lax.Precision.HIGHEST, preferred_element_type=jnp.float32)
        keep = indices != pivot
        current = jnp.where(keep[:, None] & keep[None, :], current, jnp.float32(0.0))
        factors.append(factor)
    stacked = jnp.concatenate(factors, axis=1)
    return (rows_to_slots(stacked), cols_to_slots(rows_to_slots(current)))
```

```python
import jax
import jax.numpy as jnp
from jax import lax
from jax.sharding import PartitionSpec as P

NB = 256
PANELS = 3
AXES = ("row", "col")
HIGHEST = lax.Precision.HIGHEST


def mm(a, b, dims=((1,), (0,)), precision=HIGHEST):
    return lax.dot_general(
        a, b, (dims, ((), ())), precision=precision, preferred_element_type=jnp.float32
    )


class Net:
    def __init__(self, rows, cols):
        self.rows, self.cols = rows, cols
        self.row_bits = [1 << i for i in range(1, rows.bit_length() - 1)]
        self.col_bits = [1 << i for i in range(cols.bit_length() - 1)]

    def send(self, value, target):
        pairs = []
        for r in range(self.rows):
            for c in range(self.cols):
                to = target(r, c)
                if to is not None:
                    pairs.append((r * self.cols + c, to[0] * self.cols + to[1]))
        return lax.ppermute(value, AXES, pairs)

    def core(self, value):
        return self.send(value, lambda r, c: (r ^ 1, c))

    def row_step(self, value, step):
        bits = self.row_bits
        count = len(bits)
        return self.send(
            value, lambda r, c: (r ^ bits[(step + (r & 1)) % count], c)
        )

    def col_step(self, value, bit):
        return self.send(value, lambda r, c: (r, c ^ bit))

    def row_halves(self, value, mine):
        keep = lax.dynamic_index_in_dim(value, mine, 0, keepdims=False)
        give = lax.dynamic_index_in_dim(value, 1 - mine, 0, keepdims=False)
        half = keep + self.core(give)
        for step in range(len(self.row_bits)):
            half = half + self.row_step(half, step)
        return half

    def join(self, half, mine):
        other = self.core(half)
        first = jnp.where(mine == 0, half, other)
        second = jnp.where(mine == 0, other, half)
        return jnp.stack([first, second])


def spread_rows(net, source, is_source):
    if (net.rows, net.cols) != (8, 4):
        value = jnp.where(is_source, source, 0.0)
        for bit in net.col_bits:
            value = value + net.col_step(value, bit)
        return value

    def hop(first, second):
        def target(r, c):
            up = (r // 2) % 2 == 0
            line = c if up else 3 - c
            near = (r % 2 == 0) == up
            to = (first if near else second).get(line)
            if to is None:
                return None
            return (r, to if up else 3 - to)

        return target

    got1 = net.send(source, hop({0: 1}, {1: 2}))
    got2 = net.send(got1, hop({1: 2}, {2: 3}))
    got3 = net.send(jnp.where(is_source, source, got2), hop({2: 3}, {1: 0}))
    return jnp.where(is_source, source, got1 + got2 + got3)


def invert(corner):
    lower = jnp.linalg.cholesky(corner)
    identity = jnp.eye(corner.shape[0], dtype=jnp.float32)
    return lax.linalg.triangular_solve(lower, identity, left_side=True, lower=True)


def on_device(panel, trailing):
    rows = lax.axis_size("row")
    cols = lax.axis_size("col")
    my_row = lax.axis_index("row")
    my_col = lax.axis_index("col")
    net = Net(rows, cols)
    mine = my_row % 2
    loc_rows, loc_cols = trailing.shape
    blk_rows = loc_rows // NB
    blk_cols = loc_cols // NB
    ratio = rows // cols

    strips = []
    for s in range(PANELS):
        pivot = panel[s]
        strip = lax.dynamic_slice_in_dim(trailing, (pivot // rows) * NB, NB, 0)
        strips.append(jnp.where(my_row == pivot % rows, strip, 0.0))

    blocks = []
    names = []
    for a in range(PANELS):
        for b in range(a + 1):
            piece = lax.dynamic_slice_in_dim(strips[a], (panel[b] // cols) * NB, NB, 1)
            blocks.append(jnp.where(my_col == panel[b] % cols, piece, 0.0))
            names.append((a, b))
    packed = jnp.stack(blocks).reshape(2, len(blocks) // 2, NB, NB)
    half = net.row_halves(packed, mine)
    for bit in net.col_bits:
        half = half + net.col_step(half, bit)
    packed = net.join(half, mine).reshape(len(blocks), NB, NB)
    corner = {name: packed[i] for i, name in enumerate(names)}

    is_source = my_col == my_row % cols
    col_raw, row_raw = [], []
    for s in range(PANELS):
        strip = strips[s].reshape(2, NB // 2, loc_cols)
        full = net.join(net.row_halves(strip, mine), mine).reshape(NB, loc_cols)
        col_raw.append(full)
        own = full.reshape(NB, blk_rows, ratio, NB)
        own = lax.dynamic_index_in_dim(own, my_row // cols, 2, keepdims=False)
        row_raw.append(spread_rows(net, own.reshape(NB, loc_rows), is_source))

    inverse, low = [], {}
    for s in range(PANELS):
        diag = corner[(s, s)]
        for k in range(s):
            diag = diag - mm(low[(s, k)], low[(s, k)], ((1,), (1,)))
        inverse.append(invert(diag))
        for a in range(s + 1, PANELS):
            left = corner[(a, s)]
            for k in range(s):
                left = left - mm(low[(a, k)], low[(s, k)], ((1,), (1,)))
            low[(a, s)] = mm(left, inverse[s], ((1,), (1,)))

    row_ids = jnp.arange(loc_rows, dtype=jnp.int32) // NB * rows + my_row
    col_ids = jnp.arange(loc_cols, dtype=jnp.int32) // NB * cols + my_col

    def factors(raw, ids):
        out = []
        alive = jnp.ones(ids.shape, jnp.bool_)
        for s in range(PANELS):
            left = raw[s]
            for k in range(s):
                left = left - mm(low[(s, k)], out[k])
            out.append(jnp.where(alive[None, :], mm(inverse[s], left), 0.0))
            alive = alive & (ids != panel[s])
        return out, alive

    row_factor, row_alive = factors(row_raw, row_ids)
    col_factor, col_alive = factors(col_raw, col_ids)
    row_all = jnp.concatenate(row_factor, axis=0).T
    col_all = jnp.concatenate(col_factor, axis=0)
    current = trailing - mm(row_all, col_all)
    current = jnp.where(row_alive[:, None] & col_alive[None, :], current, 0.0)
    return (row_all, current)


def solution(mesh):
    in_specs = (P(), P("row", "col"))
    out_specs = (P("row", None), P("row", "col"))
    return jax.shard_map(
        on_device, mesh=mesh, in_specs=in_specs, out_specs=out_specs, check_vma=False
    )
```

```python
import jax
import jax.numpy as jnp
from jax import lax
from jax.experimental import pallas as pl
from jax.experimental.pallas import tpu as pltpu
from jax.sharding import PartitionSpec as P

NB = 256
PANELS = 3
AXES = ("row", "col")
HIGHEST = lax.Precision.HIGHEST
HIGH = lax.Precision.HIGH
INTERPRET = False


def mm(a, b, dims=((1,), (0,)), precision=HIGHEST):
    return lax.dot_general(
        a, b, (dims, ((), ())), precision=precision, preferred_element_type=jnp.float32
    )


def kdot(a, b, ca=1, cb=0):
    return lax.dot_general(a, b, (((ca,), (cb,)), ((), ())), precision=HIGHEST,
        preferred_element_type=jnp.float32)

def iotas(shape):
    return (lax.broadcasted_iota(jnp.int32, shape, 0), lax.broadcasted_iota(jnp.int32, shape, 1))

def invert_block(d_ref, w_ref, work_ref):
    n = d_ref.shape[0]
    ii, jj = iotas((n, n))
    eye = ii == jj
    d = d_ref[...]
    diag = jnp.where(eye, d, 0.0)
    by_col = lax.rsqrt(jnp.sum(diag, axis=0, keepdims=True))
    by_row = lax.rsqrt(jnp.sum(diag, axis=1, keepdims=True))

    def half(r):
        return jnp.where(ii > jj, r, jnp.where(eye, 0.5 * r, 0.0))

    res = jnp.where(eye, 0.0, d * by_row * by_col)
    w_ref[...] = jnp.where(eye, by_row, 0.0) - half(res) * by_col

    def cond(carry):
        count, size = carry
        return (count < 12) & (size > 1e-7)

    def body(carry):
        count, _ = carry
        w = w_ref[...]
        s = kdot(kdot(w, d_ref[...]), w, 1, 1)
        res = jnp.where(eye, s - 1.0, s)
        w_ref[...] = w - kdot(half(res), w)
        return count + 1, jnp.sum(res * res)

    _, size = lax.while_loop(cond, body, (jnp.int32(0), jnp.float32(1.0)))
    low_diag = jnp.min(jnp.where(eye, w_ref[...], 1.0))

    @pl.when(jnp.logical_not((size <= 1e-7) & (low_diag > 0.0)))
    def _():
        work_ref[:, :n] = d_ref[...]
        work_ref[:, n:] = jnp.where(eye, 1.0, 0.0)
        row2, lane2 = iotas((n, 2 * n))
        row1, _ = iotas((n, 1))
        lane1 = lax.broadcasted_iota(jnp.int32, (1, 2 * n), 1)

        @pl.loop(0, n)
        def _(k):
            row = work_ref[pl.ds(k, 1), :]
            scale = lax.rsqrt(jnp.sum(jnp.where(lane1 == k, row, 0.0), axis=1, keepdims=True))
            row = row * scale
            full = work_ref[...]
            col = jnp.sum(jnp.where(lane2 == k, full, 0.0), axis=1, keepdims=True) * scale
            work_ref[...] = full - jnp.where(row1 > k, col, 0.0) * row
            work_ref[pl.ds(k, 1), :] = row
        w_ref[...] = work_ref[:, n:]

def pair(a, b):
    return a * (a + 1) // 2 + b

def chain_kernel(swap_ref, k_ref, out_ref, k_s, w_s, low_s, work_s):
    n = k_ref.shape[-1]
    for i in range(k_ref.shape[0]):
        k_s[i] = k_ref[i]
    for s in range(PANELS):
        invert_block(k_s.at[pair(s, s)], w_s.at[s], work_s)
        w = w_s[s]
        for k in range(s):
            out_ref[pair(s, k)] = kdot(w, low_s[pair(s, k)])
        h = n // 2
        @pl.when(swap_ref[0] == 0)
        def _():
            out_ref[pair(s, s)] = w
        @pl.when(swap_ref[0] != 0)
        def _():
            out_ref[pair(s, s), :, :h] = w[:, h:]
            out_ref[pair(s, s), :, h:] = w[:, :h]
        for a in range(s + 1, PANELS):
            low_s[pair(a, s)] = kdot(k_s[pair(a, s)], w, 1, 1)
        for a in range(s + 1, PANELS):
            for b in range(s + 1, a + 1):
                k_s[pair(a, b)] = k_s[pair(a, b)] - kdot(low_s[pair(a, s)], low_s[pair(b, s)], 1, 1)

def chain(swap, corner):
    count, n, _ = corner.shape
    return pl.pallas_call(
        chain_kernel,
        out_shape=jax.ShapeDtypeStruct(corner.shape, jnp.float32),
        in_specs=[pl.BlockSpec(memory_space=pltpu.SMEM), pl.BlockSpec(memory_space=pltpu.VMEM)],
        out_specs=pl.BlockSpec(memory_space=pltpu.VMEM),
        scratch_shapes=[pltpu.VMEM((count, n, n), jnp.float32), pltpu.VMEM((PANELS, n, n), jnp.float32),
                        pltpu.VMEM((count, n, n), jnp.float32), pltpu.VMEM((n, 2 * n), jnp.float32)],
        interpret=INTERPRET,
    )(swap, corner)


class Net:
    def __init__(self, rows, cols):
        self.rows, self.cols = rows, cols
        self.row_bits = [1 << i for i in range(1, rows.bit_length() - 1)]
        self.col_bits = [1 << i for i in range(cols.bit_length() - 1)]

    def send(self, value, target):
        pairs = []
        for r in range(self.rows):
            for c in range(self.cols):
                to = target(r, c)
                if to is not None:
                    pairs.append((r * self.cols + c, to[0] * self.cols + to[1]))
        return lax.ppermute(value, AXES, pairs)

    def core(self, value):
        return self.send(value, lambda r, c: (r ^ 1, c))

    def step_bit(self, step, core):
        return self.row_bits[(step + core) % len(self.row_bits)]

    def row_step(self, value, step):
        return self.send(value, lambda r, c: (r ^ self.step_bit(step, r & 1), c))

    def col_step(self, value, bit):
        return self.send(value, lambda r, c: (r, c ^ bit))

    def my_bit(self, my_row, step):
        even = (my_row // self.step_bit(step, 0)) % 2
        odd = (my_row // self.step_bit(step, 1)) % 2
        return jnp.where(my_row % 2 == 0, even, odd)


def pick(value, index):
    return lax.dynamic_index_in_dim(value, index, 0, keepdims=False)


def spread_all(net, value, my_row):
    mine = my_row % 2
    bits = [mine]
    tail = value.shape[1:]
    part = value.reshape((2, -1) + tail)
    part = pick(part, mine) + net.core(pick(part, 1 - mine))
    for step in range(len(net.row_bits)):
        bit = net.my_bit(my_row, step)
        bits.append(bit)
        part = part.reshape((2, -1) + tail)
        part = pick(part, bit) + net.row_step(pick(part, 1 - bit), step)
    for bit in net.col_bits:
        part = part + net.col_step(part, bit)
    for step in reversed(range(len(net.row_bits))):
        other = net.row_step(part, step)
        low = bits[step + 1] == 0
        part = jnp.concatenate([jnp.where(low, part, other), jnp.where(low, other, part)])
    other = net.core(part)
    low = mine == 0
    return jnp.concatenate([jnp.where(low, part, other), jnp.where(low, other, part)])


def spread_rows(net, source, is_source):
    if (net.rows, net.cols) != (8, 4):
        value = jnp.where(is_source, source, 0.0)
        for bit in net.col_bits:
            value = value + net.col_step(value, bit)
        return value

    def hop(first, second):
        def target(r, c):
            up = (r // 2) % 2 == 0
            line = c if up else 3 - c
            near = (r % 2 == 0) == up
            to = (first if near else second).get(line)
            if to is None:
                return None
            return (r, to if up else 3 - to)

        return target

    got1 = net.send(source, hop({0: 1}, {1: 2}))
    got2 = net.send(got1, hop({1: 2}, {2: 3}))
    got3 = net.send(jnp.where(is_source, source, got2), hop({2: 3}, {1: 0}))
    return jnp.where(is_source, source, got1 + got2 + got3)


def on_device(panel, trailing):
    rows = lax.axis_size("row")
    cols = lax.axis_size("col")
    my_row = lax.axis_index("row")
    my_col = lax.axis_index("col")
    net = Net(rows, cols)
    mine = my_row % 2
    loc_rows, loc_cols = trailing.shape
    blk_rows = loc_rows // NB
    ratio = rows // cols
    split = NB // 2

    blocks = []
    for a in range(PANELS):
        for b in range(a + 1):
            at = ((panel[a] // rows) * NB, (panel[b] // cols) * NB)
            piece = lax.dynamic_slice(trailing, at, (NB, NB))
            owner = (my_row == panel[a] % rows) & (my_col == panel[b] % cols)
            blocks.append(jnp.where(owner, piece, 0.0))
    count = len(blocks)
    corner = jnp.concatenate(blocks).reshape(2 * rows, -1, NB)
    corner = spread_all(net, corner, my_row).reshape(count, NB, NB)
    solved = chain(mine.reshape(1), corner)

    is_source = my_col == my_row % cols
    col_raw, row_raw = [], []
    for s in range(PANELS):
        owner = my_row == panel[s] % rows
        first = (panel[s] // rows) * NB

        def half_strip(which):
            strip = lax.dynamic_slice(trailing, (first + which * split, 0), (split, loc_cols))
            return jnp.where(owner, strip, 0.0)

        half = half_strip(mine) + net.core(half_strip(1 - mine))
        for step in range(len(net.row_bits)):
            half = half + net.row_step(half, step)
        other = net.core(half)
        col_raw.append((half, other))
        own = []
        for part in (half, other):
            cuts = []
            for i in range(blk_rows):
                at = (i * ratio + my_row // cols) * NB
                cuts.append(lax.dynamic_slice(part, (0, at), (split, NB)))
            own.append(jnp.concatenate(cuts, axis=1))
        row_raw.append(spread_rows(net, jnp.concatenate(own), is_source))

    row_ids = jnp.arange(loc_rows, dtype=jnp.int32) // NB * rows + my_row
    col_ids = jnp.arange(loc_cols, dtype=jnp.int32) // NB * cols + my_col
    row_alive = jnp.ones((loc_rows,), jnp.bool_)
    col_alive = jnp.ones((loc_cols,), jnp.bool_)
    row_fac, col_fac = [], []
    for s in range(PANELS):
        inverse = solved[pair(s, s)]
        rfac = mm(row_raw[s], inverse, ((0,), (1,)))
        cfac = mm(inverse[:, :split], col_raw[s][0]) + mm(inverse[:, split:], col_raw[s][1])
        for k in range(s):
            rfac = rfac - mm(row_fac[k], solved[pair(s, k)], ((1,), (1,)))
            cfac = cfac - mm(solved[pair(s, k)], col_fac[k])
        row_fac.append(jnp.where(row_alive[:, None], rfac, 0.0))
        col_fac.append(jnp.where(col_alive[None, :], cfac, 0.0))
        row_alive = row_alive & (row_ids != panel[s])
        col_alive = col_alive & (col_ids != panel[s])
    early = mm(jnp.concatenate(row_fac[:-1], axis=1), jnp.concatenate(col_fac[:-1]), precision=HIGH)
    current = trailing - early
    current = current - mm(row_fac[-1], col_fac[-1], precision=HIGH)
    current = jnp.where(row_alive[:, None] & col_alive[None, :], current, 0.0)
    return (jnp.concatenate(row_fac, axis=1), current)


def solution(mesh):
    in_specs = (P(), P("row", "col"))
    out_specs = (P("row", None), P("row", "col"))
    return jax.shard_map(
        on_device, mesh=mesh, in_specs=in_specs, out_specs=out_specs, check_vma=False
    )
```

```python
import jax
import jax.numpy as jnp
from jax import lax
from jax.experimental import pallas as pl
from jax.experimental.pallas import tpu as pltpu
from jax.sharding import PartitionSpec as P

NB = 256
PANELS = 3
AXES = ("row", "col")
HIGHEST = lax.Precision.HIGHEST
HIGH = lax.Precision.HIGH
INTERPRET = False


def mm(a, b, dims=((1,), (0,)), precision=HIGHEST):
    return lax.dot_general(
        a, b, (dims, ((), ())), precision=precision, preferred_element_type=jnp.float32
    )


def kdot(a, b, ca=1, cb=0):
    return lax.dot_general(a, b, (((ca,), (cb,)), ((), ())), precision=HIGHEST,
        preferred_element_type=jnp.float32)

def iotas(shape):
    return (lax.broadcasted_iota(jnp.int32, shape, 0), lax.broadcasted_iota(jnp.int32, shape, 1))

def invert_block(d_ref, w_ref, work_ref):
    n = d_ref.shape[0]
    ii, jj = iotas((n, n))
    eye = ii == jj
    d = d_ref[...]
    diag = jnp.where(eye, d, 0.0)
    by_col = lax.rsqrt(jnp.sum(diag, axis=0, keepdims=True))
    by_row = lax.rsqrt(jnp.sum(diag, axis=1, keepdims=True))

    def half(r):
        return jnp.where(ii > jj, r, jnp.where(eye, 0.5 * r, 0.0))

    res = jnp.where(eye, 0.0, d * by_row * by_col)
    w_ref[...] = jnp.where(eye, by_row, 0.0) - half(res) * by_col

    def cond(carry):
        count, size = carry
        return (count < 12) & (size > 1e-7)

    def body(carry):
        count, _ = carry
        w = w_ref[...]
        s = kdot(kdot(w, d_ref[...]), w, 1, 1)
        res = jnp.where(eye, s - 1.0, s)
        w_ref[...] = w - kdot(half(res), w)
        return count + 1, jnp.sum(res * res)

    _, size = lax.while_loop(cond, body, (jnp.int32(0), jnp.float32(1.0)))
    low_diag = jnp.min(jnp.where(eye, w_ref[...], 1.0))

    @pl.when(jnp.logical_not((size <= 1e-7) & (low_diag > 0.0)))
    def _():
        work_ref[:, :n] = d_ref[...]
        work_ref[:, n:] = jnp.where(eye, 1.0, 0.0)
        row2, lane2 = iotas((n, 2 * n))
        row1, _ = iotas((n, 1))
        lane1 = lax.broadcasted_iota(jnp.int32, (1, 2 * n), 1)

        @pl.loop(0, n)
        def _(k):
            row = work_ref[pl.ds(k, 1), :]
            scale = lax.rsqrt(jnp.sum(jnp.where(lane1 == k, row, 0.0), axis=1, keepdims=True))
            row = row * scale
            full = work_ref[...]
            col = jnp.sum(jnp.where(lane2 == k, full, 0.0), axis=1, keepdims=True) * scale
            work_ref[...] = full - jnp.where(row1 > k, col, 0.0) * row
            work_ref[pl.ds(k, 1), :] = row
        w_ref[...] = work_ref[:, n:]

def pair(a, b):
    return a * (a + 1) // 2 + b

def chain_kernel(swap_ref, k_ref, out_ref, k_s, w_s, low_s, work_s):
    n = k_ref.shape[-1]
    for i in range(k_ref.shape[0]):
        k_s[i] = k_ref[i]
    for s in range(PANELS):
        invert_block(k_s.at[pair(s, s)], w_s.at[s], work_s)
        w = w_s[s]
        for k in range(s):
            out_ref[pair(s, k)] = kdot(w, low_s[pair(s, k)])
        h = n // 2
        @pl.when(swap_ref[0] == 0)
        def _():
            out_ref[pair(s, s)] = w
        @pl.when(swap_ref[0] != 0)
        def _():
            out_ref[pair(s, s), :, :h] = w[:, h:]
            out_ref[pair(s, s), :, h:] = w[:, :h]
        for a in range(s + 1, PANELS):
            low_s[pair(a, s)] = kdot(k_s[pair(a, s)], w, 1, 1)
        for a in range(s + 1, PANELS):
            for b in range(s + 1, a + 1):
                k_s[pair(a, b)] = k_s[pair(a, b)] - kdot(low_s[pair(a, s)], low_s[pair(b, s)], 1, 1)

def chain(swap, corner):
    count, n, _ = corner.shape
    return pl.pallas_call(
        chain_kernel,
        out_shape=jax.ShapeDtypeStruct(corner.shape, jnp.float32),
        in_specs=[pl.BlockSpec(memory_space=pltpu.SMEM), pl.BlockSpec(memory_space=pltpu.VMEM)],
        out_specs=pl.BlockSpec(memory_space=pltpu.VMEM),
        scratch_shapes=[pltpu.VMEM((count, n, n), jnp.float32), pltpu.VMEM((PANELS, n, n), jnp.float32),
                        pltpu.VMEM((count, n, n), jnp.float32), pltpu.VMEM((n, 2 * n), jnp.float32)],
        interpret=INTERPRET,
    )(swap, corner)


def spec(space=pltpu.VMEM):
    return pl.BlockSpec(memory_space=space)


def f32(*shape):
    return jax.ShapeDtypeStruct(shape, jnp.float32)


def bf16(*shape):
    return jax.ShapeDtypeStruct(shape, jnp.bfloat16)


def gather_kernel(rows, cols, info, trailing, corner_keep, corner_give, *refs):
    keeps, (gives, sem) = refs[:PANELS], refs[PANELS:]
    my_row, my_col, mine = info[PANELS], info[PANELS + 1], info[PANELS + 2]
    half = NB // 2
    blk_cols = trailing.shape[1] // NB

    def copy(row, col, out):
        source = trailing.at[
            pl.ds(pl.multiple_of(row, half), half), pl.ds(pl.multiple_of(col, NB), NB)
        ]
        return pltpu.make_async_copy(source, out, sem)

    plans = []
    for a in range(PANELS):
        for b in range(a + 1):
            n = pair(a, b)
            owner = (lax.rem(info[a], rows) == my_row) & (lax.rem(info[b], cols) == my_col)
            per = PANELS * (PANELS + 1) // 4
            place = (n // per == mine, n % per)
            row, col = lax.div(info[a], rows) * NB, lax.div(info[b], cols) * NB
            for keep in (True, False):
                out = corner_keep if keep else corner_give
                jobs = [(row + h * half, col, out.at[2 * place[1] + h]) for h in range(2)]
                plans.append((place[0] == keep, owner, jobs))
    for s in range(PANELS):
        owner = lax.rem(info[s], rows) == my_row
        row = lax.div(info[s], rows) * NB
        jobs = []
        for j in range(blk_cols):
            jobs.append((row + mine * half, j * NB, keeps[s].at[j]))
            jobs.append((row + (1 - mine) * half, j * NB, gives.at[s * blk_cols + j]))
        plans.append((True, owner, jobs))
    for there, owner, jobs in plans:

        @pl.when(there & owner)
        def _():
            for job in jobs:
                copy(*job).start()

        @pl.when(there & jnp.logical_not(owner))
        def _():
            for _, _, out in jobs:
                out[...] = jnp.zeros_like(out)

    for there, owner, jobs in plans:

        @pl.when(there & owner)
        def _():
            for job in jobs:
                copy(*job).wait()


def gather(info, trailing, rows, cols):
    half = NB // 2
    blk_cols = trailing.shape[1] // NB
    part = f32(PANELS * (PANELS + 1) // 2, half, NB)
    shapes = [part, part] + [f32(blk_cols, half, NB)] * PANELS
    shapes.append(f32(PANELS * blk_cols, half, NB))
    return pl.pallas_call(
        lambda *refs: gather_kernel(rows, cols, *refs),
        out_shape=shapes,
        in_specs=[spec(pltpu.SMEM), spec(pl.ANY)],
        out_specs=[spec()] * len(shapes),
        scratch_shapes=[pltpu.SemaphoreType.DMA],
        interpret=INTERPRET,
        cost_estimate=pl.CostEstimate(flops=0, bytes_accessed=16 << 20, transcendentals=0),
    )(info, trailing)


def halves(x):
    high = x.astype(jnp.bfloat16)
    return high, (x - high.astype(jnp.float32)).astype(jnp.bfloat16)


def is_used(info, block, step):
    used = False
    for k in range(step):
        used = used | (block == info[k])
    return used


def col_kernel(s, cols, info, half, other, solved, *refs):
    before, outs = refs[:s], refs[s:]
    block = pl.program_id(0) * cols + info[PANELS + 1]
    h = NB // 2
    fac = kdot(solved[pair(s, s), :, :h], half[0]) + kdot(solved[pair(s, s), :, h:], other[0])
    for k in range(s):
        fac = fac - kdot(solved[pair(s, k)], before[k][0])
    fac = jnp.where(is_used(info, block, s), 0.0, fac)
    if len(outs) == 3:
        outs[0][0] = fac
    high, low = halves(fac)
    outs[-2][0] = high
    outs[-1][0] = low


def col_factor(s, cols, info, half, other, solved, before):
    count = half.shape[0]
    last = s == PANELS - 1
    shapes = [] if last else [f32(count, NB, NB)]
    shapes += [bf16(count, NB, NB)] * 2
    part = pl.BlockSpec((1, NB // 2, NB), lambda i: (i, 0, 0))
    whole = pl.BlockSpec((1, NB, NB), lambda i: (i, 0, 0))
    return pl.pallas_call(
        lambda *refs: col_kernel(s, cols, *refs),
        grid=(count,),
        out_shape=shapes,
        in_specs=[spec(pltpu.SMEM), part, part, spec()] + [whole] * s,
        out_specs=[whole] * len(shapes),
        interpret=INTERPRET,
        cost_estimate=pl.CostEstimate(
            flops=12 * (s + 1) * count * NB**3, bytes_accessed=8 << 20, transcendentals=0
        ),
    )(info, half, other, solved, *before)


def row_kernel(s, rows, info, raw, solved, *refs):
    before, outs = refs[: min(s, 1)], refs[min(s, 1) :]
    block = pl.program_id(0) * rows + info[PANELS]
    full = jnp.concatenate([raw[0, 0], raw[1, 0]], axis=0)
    fac = kdot(full, solved[pair(s, s)], 0, 1)
    for k in range(s):
        fac = fac - kdot(before[0][:, k * NB : (k + 1) * NB], solved[pair(s, k)], 1, 1)
    fac = jnp.where(is_used(info, block, s), 0.0, fac)
    outs[0][...] = fac
    high, low = halves(fac)
    outs[1][...] = high
    outs[2][...] = low


def row_factor(s, rows, info, raw, solved, before):
    count = raw.shape[1]
    height = count * NB
    width = PANELS * NB
    column = pl.BlockSpec((NB, NB), lambda i: (i, 0))
    return pl.pallas_call(
        lambda *refs: row_kernel(s, rows, *refs),
        grid=(count,),
        out_shape=[f32(height, width), bf16(height, NB), bf16(height, NB)],
        in_specs=[spec(pltpu.SMEM), pl.BlockSpec((2, 1, NB // 2, NB), lambda i: (0, i, 0, 0)), spec()]
        + [pl.BlockSpec((NB, width), lambda i: (i, 0))] * len(before),
        out_specs=[pl.BlockSpec((NB, NB), lambda i: (i, s)), column, column],
        input_output_aliases={3: 0} if before else {},
        interpret=INTERPRET,
        cost_estimate=pl.CostEstimate(
            flops=12 * (s + 1) * count * NB**3, bytes_accessed=8 << 20, transcendentals=0
        ),
    )(info, raw, solved, *before)


def update_kernel(last, rows, cols, info, current, *refs):
    parts, out = refs[:-1], refs[-1]
    count = len(parts) // 4
    blk_cols = parts[2].shape[0]
    dead_row = is_used(info, pl.program_id(0) * rows + info[PANELS], PANELS)
    for j in range(blk_cols):
        at = slice(j * NB, (j + 1) * NB)
        total = None
        for k in range(count):
            rhigh, rlow, chigh, clow = parts[4 * k : 4 * k + 4]
            for left, right in ((rhigh, chigh), (rhigh, clow), (rlow, chigh)):
                term = jnp.dot(left[...], right[j], preferred_element_type=jnp.float32)
                total = term if total is None else total + term
        value = current[:, at] - total
        if last:
            dead = dead_row | is_used(info, j * cols + info[PANELS + 1], PANELS)
            value = jnp.where(dead, 0.0, value)
        out[:, at] = value


def update(last, rows, cols, info, current, parts):
    height, width = current.shape
    strip = pl.BlockSpec((NB, width), lambda i: (i, 0))
    column = pl.BlockSpec((NB, NB), lambda i: (i, 0))
    specs = [column, column, spec(), spec()] * (len(parts) // 4)
    return pl.pallas_call(
        lambda *refs: update_kernel(last, rows, cols, *refs),
        grid=(height // NB,),
        out_shape=f32(height, width),
        in_specs=[spec(pltpu.SMEM), strip] + specs,
        out_specs=strip,
        input_output_aliases={1: 0} if last else {},
        interpret=INTERPRET,
        cost_estimate=pl.CostEstimate(
            flops=6 * (len(parts) // 4) * height * width * NB,
            bytes_accessed=24 << 20,
            transcendentals=0,
        ),
    )(info, current, *parts)


class Net:
    def __init__(self, rows, cols):
        self.rows, self.cols = rows, cols
        self.row_bits = [1 << i for i in range(1, rows.bit_length() - 1)]
        self.col_bits = [1 << i for i in range(cols.bit_length() - 1)]

    def send(self, value, target):
        pairs = []
        for r in range(self.rows):
            for c in range(self.cols):
                to = target(r, c)
                if to is not None:
                    pairs.append((r * self.cols + c, to[0] * self.cols + to[1]))
        return lax.ppermute(value, AXES, pairs)

    def core(self, value):
        return self.send(value, lambda r, c: (r ^ 1, c))

    def step_bit(self, step, core):
        return self.row_bits[(step + core) % len(self.row_bits)]

    def row_step(self, value, step):
        return self.send(value, lambda r, c: (r ^ self.step_bit(step, r & 1), c))

    def col_step(self, value, bit):
        return self.send(value, lambda r, c: (r, c ^ bit))

    def my_bit(self, my_row, mine, step):
        even = (my_row & self.step_bit(step, 0)) != 0
        odd = (my_row & self.step_bit(step, 1)) != 0
        return jnp.where(mine == 0, even, odd).astype(jnp.int32)


def pick(value, index):
    return lax.dynamic_index_in_dim(value, index, 0, keepdims=False)


def spread_corner(net, part, my_row, mine):
    tail = part.shape[1:]
    bits = []
    for step in range(len(net.row_bits)):
        bit = net.my_bit(my_row, mine, step)
        bits.append(bit)
        part = part.reshape((2, -1) + tail)
        part = pick(part, bit) + net.row_step(pick(part, 1 - bit), step)
    for bit in net.col_bits:
        part = part + net.col_step(part, bit)
    for step in reversed(range(len(net.row_bits))):
        other = net.row_step(part, step)
        low = bits[step] == 0
        part = jnp.concatenate([jnp.where(low, part, other), jnp.where(low, other, part)])
    other = net.core(part)
    low = mine == 0
    return jnp.concatenate([jnp.where(low, part, other), jnp.where(low, other, part)])


def spread_rows(net, source, is_source):
    if (net.rows, net.cols) != (8, 4):
        value = jnp.where(is_source, source, 0.0)
        for bit in net.col_bits:
            value = value + net.col_step(value, bit)
        return value

    def hop(first, second):
        def target(r, c):
            up = (r // 2) % 2 == 0
            line = c if up else 3 - c
            near = (r % 2 == 0) == up
            to = (first if near else second).get(line)
            if to is None:
                return None
            return (r, to if up else 3 - to)

        return target

    got1 = net.send(source, hop({0: 1}, {1: 2}))
    got2 = net.send(got1, hop({1: 2}, {2: 3}))
    got3 = net.send(jnp.where(is_source, source, got2), hop({2: 3}, {1: 0}))
    return jnp.where(is_source, source, got1 + got2 + got3)


def on_device(panel, trailing):
    rows = lax.axis_size("row")
    cols = lax.axis_size("col")
    my_row = lax.axis_index("row")
    my_col = lax.axis_index("col")
    net = Net(rows, cols)
    mine = my_row & 1
    loc_rows, loc_cols = trailing.shape
    blk_rows, blk_cols = loc_rows // NB, loc_cols // NB
    ratio = rows // cols
    half = NB // 2
    info = jnp.concatenate([panel[:PANELS], jnp.stack([my_row, my_col, mine])])

    corner, corner_give, *keeps, gives = gather(info, trailing, rows, cols)
    corner = corner + net.core(corner_give)
    corner = corner.reshape(2 * rows // 2, -1, NB)
    corner = spread_corner(net, corner, my_row, mine)
    solved = chain(info[PANELS + 2 :], corner.reshape(-1, NB, NB))

    is_source = my_col == lax.rem(my_row, cols)
    group = lax.div(my_row, cols)
    got = net.core(gives).reshape(PANELS, blk_cols, half, NB)
    parts = []
    out = ()
    for s in range(PANELS):
        part = keeps[s] + got[s]
        for step in range(len(net.row_bits)):
            part = part + net.row_step(part, step)
        parts.append((part, net.core(part)))
    col_f, stacked = [], []
    for s in range(PANELS):
        own = jnp.stack([pick_group(v, blk_rows, ratio, group) for v in parts[s]])
        raw = spread_rows(net, own, is_source)
        fac = col_factor(s, cols, info, *parts[s], solved, col_f)
        if s < PANELS - 1:
            col_f.append(fac[0])
        out, *rfac = row_factor(s, rows, info, raw, solved, [out] if s else [])
        stacked += [*rfac, *fac[-2:]]
    current = update(False, rows, cols, info, trailing, stacked[:-4])
    current = update(True, rows, cols, info, current, stacked[-4:])
    return (out, current)


def pick_group(value, blk_rows, ratio, group):
    value = value.reshape((blk_rows, ratio) + value.shape[1:])
    return lax.dynamic_index_in_dim(value, group, 1, keepdims=False)


def solution(mesh):
    in_specs = (P(), P("row", "col"))
    out_specs = (P("row", None), P("row", "col"))
    return jax.shard_map(
        on_device, mesh=mesh, in_specs=in_specs, out_specs=out_specs, check_vma=False
    )
```

```python
import jax
import jax.numpy as jnp
from jax import lax
from jax.experimental import pallas as pl
from jax.experimental.pallas import tpu as pltpu
from jax.sharding import PartitionSpec as P


NB = 256
PANELS = 3
AXES = ("row", "col")
INTERPRET = False


def thirds(x):
    high = x.astype(jnp.bfloat16)
    rest = x - high.astype(jnp.float32)
    mid = rest.astype(jnp.bfloat16)
    return high, mid, (rest - mid.astype(jnp.float32)).astype(jnp.bfloat16)


def bdot(a, b, cb):
    return lax.dot_general(
        a, b, (((1,), (cb,)), ((), ())), preferred_element_type=jnp.float32
    )


def dot6(a, b, cb=0):
    m = a.shape[0]
    a3 = jnp.concatenate(thirds(a), axis=0)
    high, mid, low = thirds(b)
    one = bdot(a3, high, cb)
    two = bdot(a3[: 2 * m], mid, cb)
    small = bdot(a3[:m], low, cb) + two[m:] + one[2 * m :]
    return (small + (two[:m] + one[m : 2 * m])) + one[:m]


def iotas(shape):
    return (lax.broadcasted_iota(jnp.int32, shape, 0), lax.broadcasted_iota(jnp.int32, shape, 1))


def invert_block(d_ref, w_ref, work_ref):
    n = d_ref.shape[0]
    ii, jj = iotas((n, n))
    eye = ii == jj
    d = d_ref[...]
    diag = jnp.where(eye, d, 0.0)
    by_col = lax.rsqrt(jnp.sum(diag, axis=0, keepdims=True))
    by_row = lax.rsqrt(jnp.sum(diag, axis=1, keepdims=True))

    def half(r):
        return jnp.where(ii > jj, r, jnp.where(eye, 0.5 * r, 0.0))

    res = jnp.where(eye, 0.0, d * by_row * by_col)
    w_ref[...] = jnp.where(eye, by_row, 0.0) - half(res) * by_col

    def cond(carry):
        count, size = carry
        return (count < 12) & (size > 1e-7)

    def body(carry):
        count, _ = carry
        w = w_ref[...]
        s = dot6(dot6(w, d_ref[...]), w, 1)
        res = jnp.where(eye, s - 1.0, s)
        w_ref[...] = w - dot6(half(res), w)
        return count + 1, jnp.sum(res * res)

    _, size = lax.while_loop(cond, body, (jnp.int32(0), jnp.float32(1.0)))
    low_diag = jnp.min(jnp.where(eye, w_ref[...], 1.0))

    @pl.when(jnp.logical_not((size <= 1e-7) & (low_diag > 0.0)))
    def _():
        work_ref[:, :n] = d_ref[...]
        work_ref[:, n:] = jnp.where(eye, 1.0, 0.0)
        _, lane2 = iotas((n, 2 * n))
        row1, _ = iotas((n, 1))
        lane1 = lax.broadcasted_iota(jnp.int32, (1, 2 * n), 1)

        @pl.loop(0, n)
        def _(k):
            row = work_ref[pl.ds(k, 1), :]
            scale = lax.rsqrt(jnp.sum(jnp.where(lane1 == k, row, 0.0), axis=1, keepdims=True))
            row = row * scale
            full = work_ref[...]
            col = jnp.sum(jnp.where(lane2 == k, full, 0.0), axis=1, keepdims=True) * scale
            work_ref[...] = full - jnp.where(row1 > k, col, 0.0) * row
            work_ref[pl.ds(k, 1), :] = row

        w_ref[...] = work_ref[:, n:]


def pair(a, b):
    return a * (a + 1) // 2 + b


def chain_kernel(swap_ref, k_ref, out_ref, k_s, w_s, low_s, work_s):
    n = k_ref.shape[-1]
    for i in range(k_ref.shape[0]):
        k_s[i] = k_ref[i]
    for s in range(PANELS):
        invert_block(k_s.at[pair(s, s)], w_s.at[s], work_s)
        w = w_s[s]
        for k in range(s):
            out_ref[pair(s, k)] = dot6(w, low_s[pair(s, k)])
        h = n // 2

        @pl.when(swap_ref[0] == 0)
        def _():
            out_ref[pair(s, s)] = w

        @pl.when(swap_ref[0] != 0)
        def _():
            out_ref[pair(s, s), :, :h] = w[:, h:]
            out_ref[pair(s, s), :, h:] = w[:, :h]

        for a in range(s + 1, PANELS):
            low_s[pair(a, s)] = dot6(k_s[pair(a, s)], w, 1)
        for a in range(s + 1, PANELS):
            for b in range(s + 1, a + 1):
                k_s[pair(a, b)] = k_s[pair(a, b)] - dot6(low_s[pair(a, s)], low_s[pair(b, s)], 1)


def chain(swap, corner):
    count, n, _ = corner.shape
    return pl.pallas_call(
        chain_kernel,
        out_shape=jax.ShapeDtypeStruct(corner.shape, jnp.float32),
        in_specs=[pl.BlockSpec(memory_space=pltpu.SMEM), pl.BlockSpec(memory_space=pltpu.VMEM)],
        out_specs=pl.BlockSpec(memory_space=pltpu.VMEM),
        scratch_shapes=[pltpu.VMEM((count, n, n), jnp.float32), pltpu.VMEM((PANELS, n, n), jnp.float32),
                        pltpu.VMEM((count, n, n), jnp.float32), pltpu.VMEM((n, 2 * n), jnp.float32)],
        interpret=INTERPRET,
    )(swap, corner)


def spec(space=pltpu.VMEM):
    return pl.BlockSpec(memory_space=space)


def f32(*shape):
    return jax.ShapeDtypeStruct(shape, jnp.float32)


def bf16(*shape):
    return jax.ShapeDtypeStruct(shape, jnp.bfloat16)


def gather_kernel(rows, cols, info, trailing, corner_keep, corner_give, *refs):
    keeps, (gives, sem) = refs[:PANELS], refs[PANELS:]
    my_row, my_col, mine = info[PANELS], info[PANELS + 1], info[PANELS + 2]
    half = NB // 2
    blk_cols = trailing.shape[1] // NB

    def copy(row, col, out):
        source = trailing.at[
            pl.ds(pl.multiple_of(row, half), half), pl.ds(pl.multiple_of(col, NB), NB)
        ]
        return pltpu.make_async_copy(source, out, sem)

    plans = []
    for a in range(PANELS):
        for b in range(a + 1):
            n = pair(a, b)
            owner = (lax.rem(info[a], rows) == my_row) & (lax.rem(info[b], cols) == my_col)
            per = PANELS * (PANELS + 1) // 4
            place = (n // per == mine, n % per)
            row, col = lax.div(info[a], rows) * NB, lax.div(info[b], cols) * NB
            for keep in (True, False):
                out = corner_keep if keep else corner_give
                jobs = [(row + h * half, col, out.at[2 * place[1] + h]) for h in range(2)]
                plans.append((place[0] == keep, owner, jobs))
    for s in range(PANELS):
        owner = lax.rem(info[s], rows) == my_row
        row = lax.div(info[s], rows) * NB
        jobs = []
        for j in range(blk_cols):
            jobs.append((row + mine * half, j * NB, keeps[s].at[j]))
            jobs.append((row + (1 - mine) * half, j * NB, gives.at[s * blk_cols + j]))
        plans.append((True, owner, jobs))
    for there, owner, jobs in plans:

        @pl.when(there & owner)
        def _():
            for job in jobs:
                copy(*job).start()

        @pl.when(there & jnp.logical_not(owner))
        def _():
            for _, _, out in jobs:
                out[...] = jnp.zeros_like(out)

    for there, owner, jobs in plans:

        @pl.when(there & owner)
        def _():
            for job in jobs:
                copy(*job).wait()


def gather(info, trailing, rows, cols):
    half = NB // 2
    blk_cols = trailing.shape[1] // NB
    part = f32(PANELS * (PANELS + 1) // 2, half, NB)
    shapes = [part, part] + [f32(blk_cols, half, NB)] * PANELS
    shapes.append(f32(PANELS * blk_cols, half, NB))
    return pl.pallas_call(
        lambda *refs: gather_kernel(rows, cols, *refs),
        out_shape=shapes,
        in_specs=[spec(pltpu.SMEM), spec(pl.ANY)],
        out_specs=[spec()] * len(shapes),
        scratch_shapes=[pltpu.SemaphoreType.DMA],
        interpret=INTERPRET,
        cost_estimate=pl.CostEstimate(flops=0, bytes_accessed=16 << 20, transcendentals=0),
    )(info, trailing)


def halves(x):
    high = x.astype(jnp.bfloat16)
    return high, (x - high.astype(jnp.float32)).astype(jnp.bfloat16)


def is_used(info, block, step):
    used = False
    for k in range(step):
        used = used | (block == info[k])
    return used


def col_kernel(s, cols, info, half, other, solved, *refs):
    before, outs = refs[:s], refs[s:]
    block = pl.program_id(0) * cols + info[PANELS + 1]
    fac = dot6(solved[pair(s, s)], jnp.concatenate([half[0], other[0]], axis=0))
    for k in range(s):
        fac = fac - dot6(solved[pair(s, k)], before[k][0])
    fac = jnp.where(is_used(info, block, s), 0.0, fac)
    if len(outs) == 3:
        outs[0][0] = fac
    high, low = halves(fac)
    outs[-2][0] = high
    outs[-1][0] = low


def col_factor(s, cols, info, half, other, solved, before):
    count = half.shape[0]
    last = s == PANELS - 1
    shapes = [] if last else [f32(count, NB, NB)]
    shapes += [bf16(count, NB, NB)] * 2
    part = pl.BlockSpec((1, NB // 2, NB), lambda i: (i, 0, 0))
    whole = pl.BlockSpec((1, NB, NB), lambda i: (i, 0, 0))
    return pl.pallas_call(
        lambda *refs: col_kernel(s, cols, *refs),
        grid=(count,),
        out_shape=shapes,
        in_specs=[spec(pltpu.SMEM), part, part, spec()] + [whole] * s,
        out_specs=[whole] * len(shapes),
        interpret=INTERPRET,
        cost_estimate=pl.CostEstimate(
            flops=12 * (s + 1) * count * NB**3, bytes_accessed=8 << 20, transcendentals=0
        ),
    )(info, half, other, solved, *before)


def row_kernel(s, rows, count, info, solved, *refs):
    sources, refs = refs[:count], refs[count:]
    before, (out, out_high, out_low, raw, sem) = refs[: min(s, 1)], refs[min(s, 1) :]
    step = pl.program_id(0)

    @pl.when(step == 0)
    def _():
        for which, source in enumerate(sources):

            @pl.when(info[PANELS + 3] == which)
            def _():
                copy = pltpu.make_async_copy(source, raw, sem)
                copy.start()
                copy.wait()

    block = step * rows + info[PANELS]
    full = jnp.concatenate([raw[0, step], raw[1, step]], axis=0)
    fac = dot6(full.T, solved[pair(s, s)], 1)
    for k in range(s):
        fac = fac - dot6(before[0][:, k * NB : (k + 1) * NB], solved[pair(s, k)], 1)
    fac = jnp.where(is_used(info, block, s), 0.0, fac)
    out[...] = fac
    out_high[...], out_low[...] = halves(fac)


def row_factor(s, rows, info, sources, solved, before):
    raw = sources[0].shape
    count = raw[1]
    height = count * NB
    width = PANELS * NB
    column = pl.BlockSpec((NB, NB), lambda i: (i, 0))
    return pl.pallas_call(
        lambda *refs: row_kernel(s, rows, len(sources), *refs),
        grid=(count,),
        out_shape=[f32(height, width), bf16(height, NB), bf16(height, NB)],
        in_specs=[spec(pltpu.SMEM), spec()]
        + [spec(pl.ANY)] * len(sources)
        + [pl.BlockSpec((NB, width), lambda i: (i, 0))] * len(before),
        out_specs=[pl.BlockSpec((NB, NB), lambda i: (i, s)), column, column],
        scratch_shapes=[pltpu.VMEM(raw, jnp.float32), pltpu.SemaphoreType.DMA],
        input_output_aliases={2 + len(sources): 0} if before else {},
        interpret=INTERPRET,
        cost_estimate=pl.CostEstimate(
            flops=12 * (s + 1) * count * NB**3, bytes_accessed=8 << 20, transcendentals=0
        ),
    )(info, solved, *sources, *before)


def own_kernel(ratio, info, half, other, out, sem):
    group = info[PANELS + 4]
    copies = []
    for h, part in enumerate((half, other)):
        for i in range(out.shape[1]):
            copies.append(
                pltpu.make_async_copy(part.at[i * ratio + group], out.at[h, i], sem)
            )
    for copy in copies:
        copy.start()
    for copy in copies:
        copy.wait()


def own_rows(ratio, info, half, other):
    return pl.pallas_call(
        lambda *refs: own_kernel(ratio, *refs),
        out_shape=f32(2, half.shape[0] // ratio, *half.shape[1:]),
        in_specs=[spec(pltpu.SMEM), spec(pl.ANY), spec(pl.ANY)],
        out_specs=spec(),
        scratch_shapes=[pltpu.SemaphoreType.DMA],
        interpret=INTERPRET,
        cost_estimate=pl.CostEstimate(flops=0, bytes_accessed=2 << 20, transcendentals=0),
    )(info, half, other)


def update_kernel(last, rows, cols, info, current, *refs):
    parts, out = refs[:-1], refs[-1]
    total = None
    for k in range(len(parts) // 4):
        rhigh, rlow, chigh, clow = parts[4 * k : 4 * k + 4]
        for left, right in ((rhigh, clow), (rlow, chigh), (rhigh, chigh)):
            term = jnp.dot(left[...], right[0], preferred_element_type=jnp.float32)
            total = term if total is None else total + term
    value = current[...] - total
    if not last:
        out[...] = value
        return
    dead = is_used(info, pl.program_id(0) * cols + info[PANELS + 1], PANELS)
    for i in range(value.shape[0] // NB):
        used = dead | is_used(info, i * rows + info[PANELS], PANELS)
        at = slice(i * NB, (i + 1) * NB)
        out[at, :] = jnp.where(used, 0.0, value[at])


def update(last, rows, cols, info, current, parts):
    height, width = current.shape
    strip = pl.BlockSpec((height, NB), lambda i: (0, i))
    block = pl.BlockSpec((1, NB, NB), lambda i: (i, 0, 0))
    return pl.pallas_call(
        lambda *refs: update_kernel(last, rows, cols, *refs),
        grid=(width // NB,),
        out_shape=f32(height, width),
        in_specs=[spec(pltpu.SMEM), strip] + [spec(), spec(), block, block] * (len(parts) // 4),
        out_specs=strip,
        input_output_aliases={1: 0} if last else {},
        interpret=INTERPRET,
        cost_estimate=pl.CostEstimate(
            flops=6 * (len(parts) // 4) * height * width * NB,
            bytes_accessed=24 << 20,
            transcendentals=0,
        ),
    )(info, current, *parts)


class Net:
    def __init__(self, rows, cols):
        self.rows, self.cols = rows, cols
        self.row_bits = [1 << i for i in range(1, rows.bit_length() - 1)]
        self.col_bits = [1 << i for i in range(cols.bit_length() - 1)]

    def send(self, value, target):
        pairs = []
        for r in range(self.rows):
            for c in range(self.cols):
                to = target(r, c)
                if to is not None:
                    pairs.append((r * self.cols + c, to[0] * self.cols + to[1]))
        return lax.ppermute(value, AXES, pairs)

    def core(self, value):
        return self.send(value, lambda r, c: (r ^ 1, c))

    def step_bit(self, step, core):
        return self.row_bits[(step + core) % len(self.row_bits)]

    def row_step(self, value, step, turn=0):
        return self.send(value, lambda r, c: (r ^ self.step_bit(step, (r + turn) & 1), c))

    def col_step(self, value, bit):
        return self.send(value, lambda r, c: (r, c ^ bit))

    def my_bit(self, my_row, mine, step, turn):
        even = (my_row & self.step_bit(step, turn)) != 0
        odd = (my_row & self.step_bit(step, 1 - turn)) != 0
        return jnp.where(mine == 0, even, odd).astype(jnp.int32)


def pick(value, index):
    return lax.dynamic_index_in_dim(value, index, 0, keepdims=False)


def spread_corner(net, part, my_row, mine):
    tail = part.shape[1:]
    bits = []
    turn = 1
    for step in range(len(net.row_bits)):
        bit = net.my_bit(my_row, mine, step, turn)
        bits.append(bit)
        part = part.reshape((2, -1) + tail)
        part = pick(part, bit) + net.row_step(pick(part, 1 - bit), step, turn)
    for bit in net.col_bits:
        part = part + net.col_step(part, bit)
    for step in reversed(range(len(net.row_bits))):
        other = net.row_step(part, step, turn)
        low = bits[step] == 0
        part = jnp.concatenate([jnp.where(low, part, other), jnp.where(low, other, part)])
    other = net.core(part)
    low = mine == 0
    return jnp.concatenate([jnp.where(low, part, other), jnp.where(low, other, part)])


def spread_rows(net, source, is_source):
    if (net.rows, net.cols) != (8, 4):
        value = jnp.where(is_source, source, 0.0)
        for bit in net.col_bits:
            value = value + net.col_step(value, bit)
        return [value]

    def hop(first, second):
        def target(r, c):
            up = (r // 2) % 2 == 0
            line = c if up else 3 - c
            near = (r % 2 == 0) == up
            to = (first if near else second).get(line)
            if to is None:
                return None
            return (r, to if up else 3 - to)

        return target

    got1 = net.send(source, hop({0: 1}, {1: 2}))
    got2 = net.send(got1, hop({1: 2}, {2: 3}))
    third = jnp.where(is_source, source, got2)
    got3 = net.send(third, hop({2: 3}, {1: 0}))
    return [source, got1, got2, got3]


def source_code(net, my_row, my_col):
    if (net.rows, net.cols) != (8, 4):
        return jnp.int32(0)
    up = (my_row & 2) == 0
    line = jnp.where(up, my_col, 3 - my_col)
    near = ((my_row & 1) == 0) == up
    return jnp.where(near, line, (line + 3) & 3)


def run(panel, trailing):
    rows = lax.axis_size("row")
    cols = lax.axis_size("col")
    my_row = lax.axis_index("row")
    my_col = lax.axis_index("col")
    net = Net(rows, cols)
    mine = my_row & 1
    _, loc_cols = trailing.shape
    blk_cols = loc_cols // NB
    ratio = rows // cols
    half = NB // 2
    group = lax.div(my_row, cols)
    code = source_code(net, my_row, my_col)
    extra = jnp.stack([my_row, my_col, mine, code, group])
    info = jnp.concatenate([panel[:PANELS], extra])
    is_source = my_col == lax.rem(my_row, cols)

    corner, corner_give, *keeps, gives = gather(info, trailing, rows, cols)
    got = net.core(gives).reshape(PANELS, blk_cols, half, NB)
    corner = corner + net.core(corner_give)
    corner = spread_corner(net, corner.reshape(rows, -1, NB), my_row, mine)
    solved = chain(info[PANELS + 2 : PANELS + 3], corner.reshape(-1, NB, NB))

    parts, sources = [], []
    for s in range(PANELS):
        part = keeps[s] + got[s]
        for step in range(len(net.row_bits)):
            part = part + net.row_step(part, step)
        parts.append((part, net.core(part)))
        own = own_rows(ratio, info, *parts[s])
        sources.append(spread_rows(net, own, is_source))
    out, col_f, stacked = (), [], []
    for s in range(PANELS):
        fac = col_factor(s, cols, info, *parts[s], solved, col_f)
        if s < PANELS - 1:
            col_f.append(fac[0])
        out, *rfac = row_factor(s, rows, info, sources[s], solved, [out] if s else [])
        stacked += [*rfac, *fac[-2:]]
    current = update(False, rows, cols, info, trailing, stacked[:-4])
    current = update(True, rows, cols, info, current, stacked[-4:])
    return (out, current)


def solution(mesh):
    in_specs = (P(), P("row", "col"))
    out_specs = (P("row", None), P("row", "col"))
    return jax.shard_map(run, mesh=mesh, in_specs=in_specs, out_specs=out_specs, check_vma=False)
```

```python
import jax
import jax.numpy as jnp
from jax import lax
from jax.experimental import pallas as pl
from jax.experimental.pallas import tpu as pltpu
from jax.sharding import PartitionSpec as P


NB = 256
PANELS = 3
AXES = ("row", "col")
INTERPRET = False
VMEM_LIMIT = 24 << 20


def thirds(x):
    high = x.astype(jnp.bfloat16)
    rest = x - high.astype(jnp.float32)
    mid = rest.astype(jnp.bfloat16)
    return high, mid, (rest - mid.astype(jnp.float32)).astype(jnp.bfloat16)


def dot6(a, b, cb=0):
    ah, am, al = thirds(a)
    bh, bm, bl = thirds(b)
    left = jnp.concatenate([am, al, ah, am, ah, ah], axis=1)
    right = jnp.concatenate([bm, bh, bl, bh, bm, bh], axis=cb)
    return lax.dot_general(
        left, right, (((1,), (cb,)), ((), ())), preferred_element_type=jnp.float32
    )


def iotas(shape):
    return (lax.broadcasted_iota(jnp.int32, shape, 0), lax.broadcasted_iota(jnp.int32, shape, 1))


def invert_block(d_ref, w_ref, work_ref):
    n = d_ref.shape[0]
    ii, jj = iotas((n, n))
    eye = ii == jj
    d = d_ref[...]
    diag = jnp.where(eye, d, 0.0)
    by_col = lax.rsqrt(jnp.sum(diag, axis=0, keepdims=True))
    by_row = lax.rsqrt(jnp.sum(diag, axis=1, keepdims=True))

    def half(r):
        return jnp.where(ii > jj, r, jnp.where(eye, 0.5 * r, 0.0))

    res = jnp.where(eye, 0.0, d * by_row * by_col)
    w_ref[...] = jnp.where(eye, by_row, 0.0) - half(res) * by_col

    def cond(carry):
        count, size = carry
        return (count < 12) & (size > 1e-7)

    def body(carry):
        count, _ = carry
        w = w_ref[...]
        s = dot6(dot6(w, d_ref[...]), w, 1)
        res = jnp.where(eye, s - 1.0, s)
        w_ref[...] = w - dot6(half(res), w)
        return count + 1, jnp.sum(res * res)

    _, size = lax.while_loop(cond, body, (jnp.int32(0), jnp.float32(1.0)))
    low_diag = jnp.min(jnp.where(eye, w_ref[...], 1.0))

    @pl.when(jnp.logical_not((size <= 1e-7) & (low_diag > 0.0)))
    def _():
        work_ref[:, :n] = d_ref[...]
        work_ref[:, n:] = jnp.where(eye, 1.0, 0.0)
        _, lane2 = iotas((n, 2 * n))
        row1, _ = iotas((n, 1))
        lane1 = lax.broadcasted_iota(jnp.int32, (1, 2 * n), 1)

        @pl.loop(0, n)
        def _(k):
            row = work_ref[pl.ds(k, 1), :]
            scale = lax.rsqrt(jnp.sum(jnp.where(lane1 == k, row, 0.0), axis=1, keepdims=True))
            row = row * scale
            full = work_ref[...]
            col = jnp.sum(jnp.where(lane2 == k, full, 0.0), axis=1, keepdims=True) * scale
            work_ref[...] = full - jnp.where(row1 > k, col, 0.0) * row
            work_ref[pl.ds(k, 1), :] = row

        w_ref[...] = work_ref[:, n:]


def pair(a, b):
    return a * (a + 1) // 2 + b


def chain_kernel(swap_ref, k_ref, out_ref, k_s, w_s, low_s, work_s):
    n = k_ref.shape[-1]
    for i in range(k_ref.shape[0]):
        k_s[i] = k_ref[i]
    for s in range(PANELS):
        invert_block(k_s.at[pair(s, s)], w_s.at[s], work_s)
        w = w_s[s]
        for k in range(s):
            out_ref[pair(s, k)] = dot6(w, low_s[pair(s, k)])
        h = n // 2

        @pl.when(swap_ref[0] == 0)
        def _():
            out_ref[pair(s, s)] = w

        @pl.when(swap_ref[0] != 0)
        def _():
            out_ref[pair(s, s), :, :h] = w[:, h:]
            out_ref[pair(s, s), :, h:] = w[:, :h]

        for a in range(s + 1, PANELS):
            low_s[pair(a, s)] = dot6(k_s[pair(a, s)], w, 1)
        for a in range(s + 1, PANELS):
            for b in range(s + 1, a + 1):
                k_s[pair(a, b)] = k_s[pair(a, b)] - dot6(low_s[pair(a, s)], low_s[pair(b, s)], 1)


def chain(swap, corner):
    count, n, _ = corner.shape
    return pl.pallas_call(
        chain_kernel,
        out_shape=jax.ShapeDtypeStruct(corner.shape, jnp.float32),
        in_specs=[pl.BlockSpec(memory_space=pltpu.SMEM), pl.BlockSpec(memory_space=pltpu.VMEM)],
        out_specs=pl.BlockSpec(memory_space=pltpu.VMEM),
        scratch_shapes=[pltpu.VMEM((count, n, n), jnp.float32), pltpu.VMEM((PANELS, n, n), jnp.float32),
                        pltpu.VMEM((count, n, n), jnp.float32), pltpu.VMEM((n, 2 * n), jnp.float32)],
        interpret=INTERPRET,
    )(swap, corner)


def spec(space=pltpu.VMEM):
    return pl.BlockSpec(memory_space=space)


def f32(*shape):
    return jax.ShapeDtypeStruct(shape, jnp.float32)


def bf16(*shape):
    return jax.ShapeDtypeStruct(shape, jnp.bfloat16)


def gather_kernel(rows, cols, info, trailing, corner_keep, corner_give, *refs):
    keeps, (gives, sem) = refs[:PANELS], refs[PANELS:]
    my_row, my_col, mine = info[PANELS], info[PANELS + 1], info[PANELS + 2]
    half = NB // 2
    blk_cols = trailing.shape[1] // NB

    def copy(row, col, out):
        source = trailing.at[
            pl.ds(pl.multiple_of(row, half), half), pl.ds(pl.multiple_of(col, NB), NB)
        ]
        return pltpu.make_async_copy(source, out, sem)

    plans = []
    for a in range(PANELS):
        for b in range(a + 1):
            n = pair(a, b)
            owner = (lax.rem(info[a], rows) == my_row) & (lax.rem(info[b], cols) == my_col)
            per = PANELS * (PANELS + 1) // 4
            place = (n // per == mine, n % per)
            row, col = lax.div(info[a], rows) * NB, lax.div(info[b], cols) * NB
            for keep in (True, False):
                out = corner_keep if keep else corner_give
                jobs = [(row + h * half, col, out.at[2 * place[1] + h]) for h in range(2)]
                plans.append((place[0] == keep, owner, jobs))
    for s in range(PANELS):
        owner = lax.rem(info[s], rows) == my_row
        row = lax.div(info[s], rows) * NB
        jobs = []
        for j in range(blk_cols):
            jobs.append((row + mine * half, j * NB, keeps[s].at[j]))
            jobs.append((row + (1 - mine) * half, j * NB, gives.at[s * blk_cols + j]))
        plans.append((True, owner, jobs))
    for there, owner, jobs in plans:

        @pl.when(there & owner)
        def _():
            for job in jobs:
                copy(*job).start()

        @pl.when(there & jnp.logical_not(owner))
        def _():
            for _, _, out in jobs:
                out[...] = jnp.zeros_like(out)

    for there, owner, jobs in plans:

        @pl.when(there & owner)
        def _():
            for job in jobs:
                copy(*job).wait()


def gather(info, trailing, rows, cols):
    half = NB // 2
    blk_cols = trailing.shape[1] // NB
    part = f32(PANELS * (PANELS + 1) // 2, half, NB)
    shapes = [part, part] + [f32(blk_cols, half, NB)] * PANELS
    shapes.append(f32(PANELS * blk_cols, half, NB))
    return pl.pallas_call(
        lambda *refs: gather_kernel(rows, cols, *refs),
        out_shape=shapes,
        in_specs=[spec(pltpu.SMEM), spec(pl.ANY)],
        out_specs=[spec()] * len(shapes),
        scratch_shapes=[pltpu.SemaphoreType.DMA],
        interpret=INTERPRET,
        cost_estimate=pl.CostEstimate(flops=0, bytes_accessed=16 << 20, transcendentals=0),
    )(info, trailing)


def halves(x):
    high = x.astype(jnp.bfloat16)
    return high, (x - high.astype(jnp.float32)).astype(jnp.bfloat16)


def is_used(info, block, step):
    used = False
    for k in range(step):
        used = used | (block == info[k])
    return used


def params():
    return pltpu.CompilerParams(vmem_limit_bytes=VMEM_LIMIT)


def cost(flops, mib):
    return pl.CostEstimate(flops=flops, bytes_accessed=mib << 20, transcendentals=0)


def block_of(name):
    return pl.BlockSpec((1, NB, NB), lambda i: (pair(*name), 0, 0))


def col_kernel(cols, info, *refs):
    raw, solved, (parts, rest) = refs[: 2 * PANELS - 2], refs[2 * PANELS - 2 : -2], refs[-2:]
    block = pl.program_id(0) * cols + info[PANELS + 1]
    facs = []
    last = PANELS - 1
    for s in range(last):
        full = jnp.concatenate([raw[2 * s][0], raw[2 * s + 1][0]], axis=0)
        fac = dot6(solved[pair(s, s)][0], full)
        for k in range(s):
            fac = fac - dot6(solved[pair(s, k)][0], facs[k])
        facs.append(jnp.where(is_used(info, block, s), 0.0, fac))
        for i, part in enumerate(halves(facs[s])):
            at = (2 * s + i) * NB
            parts[0, at : at + NB] = part
    total = None
    for k in range(last):
        term = dot6(solved[pair(last, k)][0], facs[k])
        total = term if total is None else total + term
    rest[0] = total


def col_factor(cols, info, raw, solved):
    count = raw[0].shape[0]
    last = PANELS - 1
    names = [(a, b) for a in range(PANELS) for b in range(a + 1)][:-1]
    part = pl.BlockSpec((1, NB // 2, NB), lambda i: (i, 0, 0))
    return pl.pallas_call(
        lambda *refs: col_kernel(cols, *refs),
        grid=(count,),
        out_shape=[bf16(count, 2 * last * NB, NB), f32(count, NB, NB)],
        in_specs=[spec(pltpu.SMEM)] + [part] * len(raw) + [block_of(n) for n in names],
        out_specs=[
            pl.BlockSpec((1, 2 * last * NB, NB), lambda i: (i, 0, 0)),
            pl.BlockSpec((1, NB, NB), lambda i: (i, 0, 0)),
        ],
        compiler_params=params(),
        interpret=INTERPRET,
        cost_estimate=cost(60 * count * NB**3, 12),
    )(info, *raw, *[solved] * len(names))


def fetch(info, sources, raw, sem):
    for which, source in enumerate(sources):

        @pl.when(info[PANELS + 3] == which)
        def _():
            copy = pltpu.make_async_copy(source, raw, sem)
            copy.start()
            copy.wait()


def row_kernel(s, rows, count, info, *refs):
    sources, refs = refs[:count], refs[count:]
    last = PANELS - 1
    total = (s + 1) + (PANELS - 1 if s == last - 1 else 0)
    solved, refs = refs[:total], refs[total:]
    before, refs = refs[:s], refs[s:]
    out, parts, raw, sem = refs[0], refs[1], refs[-2], refs[-1]
    step = pl.program_id(0)

    @pl.when(step == 0)
    def _():
        fetch(info, sources, raw, sem)

    full = jnp.concatenate([raw[0, step], raw[1, step]], axis=0)
    fac = dot6(full.T, solved[s][0], 1)
    facs = [ref[...] for ref in before]
    for k in range(s):
        fac = fac - dot6(facs[k], solved[k][0], 1)
    fac = jnp.where(is_used(info, step * rows + info[PANELS], s), 0.0, fac)
    out[...] = fac
    for i, part in enumerate(halves(fac)):
        parts[:, i * NB : (i + 1) * NB] = part
    if s == last - 1:
        facs.append(fac)
        rest = None
        for k in range(last):
            term = dot6(facs[k], solved[s + 1 + k][0], 1)
            rest = term if rest is None else rest + term
        refs[2][...] = rest


def row_factor(s, rows, info, sources, solved, before):
    raw = sources[0].shape
    count = raw[1]
    height = count * NB
    names = [(s, k) for k in range(s + 1)]
    shapes = [f32(height, PANELS * NB), bf16(height, 2 * NB)]
    specs = [
        pl.BlockSpec((NB, NB), lambda i: (i, s)),
        pl.BlockSpec((NB, 2 * NB), lambda i: (i, 0)),
    ]
    if s == PANELS - 2:
        names += [(PANELS - 1, k) for k in range(PANELS - 1)]
        shapes.append(f32(height, NB))
        specs.append(pl.BlockSpec((NB, NB), lambda i: (i, 0)))

    def column(k):
        return pl.BlockSpec((NB, NB), lambda i: (i, k))

    return pl.pallas_call(
        lambda *refs: row_kernel(s, rows, len(sources), *refs),
        grid=(count,),
        out_shape=shapes,
        in_specs=[spec(pltpu.SMEM)]
        + [spec(pl.ANY)] * len(sources)
        + [block_of(n) for n in names]
        + [column(k) for k in range(s)],
        out_specs=specs,
        scratch_shapes=[pltpu.VMEM(raw, jnp.float32), pltpu.SemaphoreType.DMA],
        input_output_aliases={1 + len(sources) + len(names): 0} if s else {},
        compiler_params=params(),
        interpret=INTERPRET,
        cost_estimate=cost(12 * len(names) * count * NB**3, 8),
    )(info, *sources, *[solved] * len(names), *before * s)


def own_kernel(ratio, info, half, other, out, sem):
    group = info[PANELS + 4]
    copies = []
    for h, part in enumerate((half, other)):
        for i in range(out.shape[1]):
            copies.append(
                pltpu.make_async_copy(part.at[i * ratio + group], out.at[h, i], sem)
            )
    for copy in copies:
        copy.start()
    for copy in copies:
        copy.wait()


def own_rows(ratio, info, half, other):
    return pl.pallas_call(
        lambda *refs: own_kernel(ratio, *refs),
        out_shape=f32(2, half.shape[0] // ratio, *half.shape[1:]),
        in_specs=[spec(pltpu.SMEM), spec(pl.ANY), spec(pl.ANY)],
        out_specs=spec(),
        scratch_shapes=[pltpu.SemaphoreType.DMA],
        interpret=INTERPRET,
        cost_estimate=pl.CostEstimate(flops=0, bytes_accessed=2 << 20, transcendentals=0),
    )(info, half, other)


def set_left(left, parts):
    for k, part in enumerate(parts):
        for i, at in enumerate((0, 1, 0)):
            to = (3 * k + i) * NB
            left[:, to : to + NB] = part[:, at * NB : (at + 1) * NB]


def early_kernel(info, current, cparts, *refs):
    rparts, out, left = refs[:-2], refs[-2], refs[-1]

    @pl.when(pl.program_id(0) == 0)
    def _():
        set_left(left, rparts)

    blocks = []
    for k in range(len(rparts)):
        high = cparts[0, 2 * k * NB : (2 * k + 1) * NB]
        low = cparts[0, (2 * k + 1) * NB : (2 * k + 2) * NB]
        blocks += [low, high, high]
    right = jnp.concatenate(blocks, axis=0)
    out[...] = current[...] - jnp.dot(left[...], right, preferred_element_type=jnp.float32)


def early_update(info, current, cparts, rparts):
    height, width = current.shape
    strip = pl.BlockSpec((height, NB), lambda i: (0, i))
    return pl.pallas_call(
        early_kernel,
        grid=(width // NB,),
        out_shape=f32(height, width),
        in_specs=[
            spec(pltpu.SMEM),
            strip,
            pl.BlockSpec((1,) + cparts.shape[1:], lambda i: (i, 0, 0)),
        ]
        + [spec()] * len(rparts),
        out_specs=strip,
        scratch_shapes=[pltpu.VMEM((height, 3 * len(rparts) * NB), jnp.bfloat16)],
        compiler_params=params(),
        interpret=INTERPRET,
        cost_estimate=cost(12 * height * width * NB, 24),
    )(info, current, cparts, *rparts)


def last_kernel(rows, cols, count, info, *refs):
    sources, refs = refs[:count], refs[count:]
    current, half, other, rest, w, row_rest, _, out, fout = refs[:9]
    raw, fac_s, parts, left, sem, out_sem = refs[9:]
    last = PANELS - 1
    step = pl.program_id(0)
    blk_rows = raw.shape[1]
    write = pltpu.make_async_copy(fac_s, fout.at[:, pl.ds(last * NB, NB)], out_sem)

    @pl.when(step == 0)
    def _():
        fetch(info, sources, raw, sem)
        for i in range(blk_rows):
            at = slice(i * NB, (i + 1) * NB)
            full = jnp.concatenate([raw[0, i], raw[1, i]], axis=0)
            fac = dot6(full.T, w[0], 1) - row_rest[at]
            fac = jnp.where(is_used(info, i * rows + info[PANELS], last), 0.0, fac)
            fac_s[at] = fac
            high, low = halves(fac)
            parts[at, :NB] = high
            parts[at, NB:] = low
        set_left(left, [parts])

    @pl.when(step == 1)
    def _():
        write.start()

    block = step * cols + info[PANELS + 1]
    fac = dot6(w[0], jnp.concatenate([half[0], other[0]], axis=0)) - rest[0]
    high, low = halves(jnp.where(is_used(info, block, last), 0.0, fac))
    right = jnp.concatenate([low, high, high], axis=0)
    value = current[...] - jnp.dot(left[...], right, preferred_element_type=jnp.float32)
    dead = is_used(info, block, PANELS)
    for i in range(blk_rows):
        used = dead | is_used(info, i * rows + info[PANELS], PANELS)
        at = slice(i * NB, (i + 1) * NB)
        out[at, :] = jnp.where(used, 0.0, value[at])

    @pl.when(step == pl.num_programs(0) - 1)
    def _():
        write.wait()


def last_update(rows, cols, info, sources, current, raw, rest, solved, row_rest, out):
    height, width = current.shape
    strip = pl.BlockSpec((height, NB), lambda i: (0, i))
    part = pl.BlockSpec((1, NB // 2, NB), lambda i: (i, 0, 0))
    last = PANELS - 1
    count = len(sources)
    return pl.pallas_call(
        lambda *refs: last_kernel(rows, cols, count, *refs),
        grid=(width // NB,),
        out_shape=[f32(height, width), f32(*out.shape)],
        in_specs=[spec(pltpu.SMEM)]
        + [spec(pl.ANY)] * count
        + [strip, part, part, pl.BlockSpec((1, NB, NB), lambda i: (i, 0, 0))]
        + [block_of((last, last)), spec(), spec(pl.ANY)],
        out_specs=[strip, spec(pl.ANY)],
        scratch_shapes=[
            pltpu.VMEM(sources[0].shape, jnp.float32),
            pltpu.VMEM((height, NB), jnp.float32),
            pltpu.VMEM((height, 2 * NB), jnp.bfloat16),
            pltpu.VMEM((height, 3 * NB), jnp.bfloat16),
            pltpu.SemaphoreType.DMA,
            pltpu.SemaphoreType.DMA,
        ],
        input_output_aliases={count + 7: 1},
        compiler_params=params(),
        interpret=INTERPRET,
        cost_estimate=cost(6 * height * width * NB, 24),
    )(info, *sources, current, *raw, rest, solved, row_rest, out)


class Net:
    def __init__(self, rows, cols):
        self.rows, self.cols = rows, cols
        self.row_bits = [1 << i for i in range(1, rows.bit_length() - 1)]
        self.col_bits = [1 << i for i in range(cols.bit_length() - 1)]

    def send(self, value, target):
        pairs = []
        for r in range(self.rows):
            for c in range(self.cols):
                to = target(r, c)
                if to is not None:
                    pairs.append((r * self.cols + c, to[0] * self.cols + to[1]))
        return lax.ppermute(value, AXES, pairs)

    def core(self, value):
        return self.send(value, lambda r, c: (r ^ 1, c))

    def step_bit(self, step, core):
        return self.row_bits[(step + core) % len(self.row_bits)]

    def row_step(self, value, step, turn=0):
        return self.send(value, lambda r, c: (r ^ self.step_bit(step, (r + turn) & 1), c))

    def col_step(self, value, bit):
        return self.send(value, lambda r, c: (r, c ^ bit))

    def my_bit(self, my_row, mine, step, turn):
        even = (my_row & self.step_bit(step, turn)) != 0
        odd = (my_row & self.step_bit(step, 1 - turn)) != 0
        return jnp.where(mine == 0, even, odd).astype(jnp.int32)


def pick(value, index):
    return lax.dynamic_index_in_dim(value, index, 0, keepdims=False)


def spread_corner(net, part, my_row, mine):
    tail = part.shape[1:]
    bits = []
    turn = 0
    for step in range(len(net.row_bits)):
        bit = net.my_bit(my_row, mine, step, turn)
        bits.append(bit)
        part = part.reshape((2, -1) + tail)
        part = pick(part, bit) + net.row_step(pick(part, 1 - bit), step, turn)
    for bit in net.col_bits:
        part = part + net.col_step(part, bit)
    for step in reversed(range(len(net.row_bits))):
        other = net.row_step(part, step, turn)
        low = bits[step] == 0
        part = jnp.concatenate([jnp.where(low, part, other), jnp.where(low, other, part)])
    other = net.core(part)
    low = mine == 0
    return jnp.concatenate([jnp.where(low, part, other), jnp.where(low, other, part)])


def spread_rows(net, source, is_source):
    if (net.rows, net.cols) != (8, 4):
        value = jnp.where(is_source, source, 0.0)
        for bit in net.col_bits:
            value = value + net.col_step(value, bit)
        return [value]

    def hop(first, second):
        def target(r, c):
            up = (r // 2) % 2 == 0
            line = c if up else 3 - c
            near = (r % 2 == 0) == up
            to = (first if near else second).get(line)
            if to is None:
                return None
            return (r, to if up else 3 - to)

        return target

    got1 = net.send(source, hop({0: 1}, {1: 2}))
    got2 = net.send(got1, hop({1: 2}, {2: 3}))
    third = jnp.where(is_source, source, got2)
    got3 = net.send(third, hop({2: 3}, {1: 0}))
    return [source, got1, got2, got3]


def source_code(net, my_row, my_col):
    if (net.rows, net.cols) != (8, 4):
        return jnp.int32(0)
    up = (my_row & 2) == 0
    line = jnp.where(up, my_col, 3 - my_col)
    near = ((my_row & 1) == 0) == up
    return jnp.where(near, line, (line + 3) & 3)


def run(panel, trailing):
    rows = lax.axis_size("row")
    cols = lax.axis_size("col")
    my_row = lax.axis_index("row")
    my_col = lax.axis_index("col")
    net = Net(rows, cols)
    mine = my_row & 1
    _, loc_cols = trailing.shape
    blk_cols = loc_cols // NB
    ratio = rows // cols
    half = NB // 2
    group = lax.div(my_row, cols)
    code = source_code(net, my_row, my_col)
    extra = jnp.stack([my_row, my_col, mine, code, group])
    info = jnp.concatenate([panel[:PANELS], extra])
    is_source = my_col == lax.rem(my_row, cols)

    corner, corner_give, *keeps, gives = gather(info, trailing, rows, cols)
    got = net.core(gives).reshape(PANELS, blk_cols, half, NB)
    corner = corner + net.core(corner_give)
    corner = spread_corner(net, corner.reshape(rows, -1, NB), my_row, mine)
    solved = chain(info[PANELS + 2 : PANELS + 3], corner.reshape(-1, NB, NB))

    parts, sources = [], []
    for s in range(PANELS):
        part = keeps[s] + got[s]
        for step in range(len(net.row_bits)):
            part = part + net.row_step(part, step)
        parts.append((part, net.core(part)))
        own = own_rows(ratio, info, *parts[s])
        sources.append(spread_rows(net, own, is_source))
    cparts, col_rest = col_factor(cols, info, [v for p in parts[:-1] for v in p], solved)
    out, rparts = (), []
    for s in range(PANELS - 1):
        out, *got = row_factor(s, rows, info, sources[s], solved, [out])
        rparts.append(got[0])
    current = early_update(info, trailing, cparts, rparts)
    current, out = last_update(
        rows, cols, info, sources[-1], current, parts[-1], col_rest, solved, got[1], out
    )
    return (out, current)


def solution(mesh):
    in_specs = (P(), P("row", "col"))
    out_specs = (P("row", None), P("row", "col"))
    return jax.shard_map(run, mesh=mesh, in_specs=in_specs, out_specs=out_specs, check_vma=False)
```

```python
import jax
import jax.numpy as jnp
from jax import lax
from jax.experimental import pallas as pl
from jax.experimental.pallas import tpu as pltpu
from jax.sharding import PartitionSpec as P


NB = 256
PANELS = 3
AXES = ("row", "col")
INTERPRET = False
VMEM_LIMIT = 24 << 20


def thirds(x):
    high = x.astype(jnp.bfloat16)
    rest = x - high.astype(jnp.float32)
    mid = rest.astype(jnp.bfloat16)
    return high, mid, (rest - mid.astype(jnp.float32)).astype(jnp.bfloat16)


def left6(a):
    high, mid, low = thirds(a)
    return jnp.concatenate([mid, low, high, mid, high, high], axis=1)


def right6(b, axis=0):
    high, mid, low = thirds(b)
    return jnp.concatenate([mid, high, low, high, mid, high], axis=axis)


def bdot(left, right, axis=0):
    return lax.dot_general(
        left, right, (((1,), (axis,)), ((), ())), preferred_element_type=jnp.float32
    )


def dot6(a, b, axis=0):
    return bdot(left6(a), right6(b, axis), axis)


def iotas(shape):
    return (lax.broadcasted_iota(jnp.int32, shape, 0), lax.broadcasted_iota(jnp.int32, shape, 1))


def invert_block(d_ref, w_ref, work_ref):
    n = d_ref.shape[0]
    ii, jj = iotas((n, n))
    eye = ii == jj
    d = d_ref[...]
    diag = jnp.where(eye, d, 0.0)
    by_col = lax.rsqrt(jnp.sum(diag, axis=0, keepdims=True))
    by_row = lax.rsqrt(jnp.sum(diag, axis=1, keepdims=True))

    def half(r):
        return jnp.where(ii > jj, r, jnp.where(eye, 0.5 * r, 0.0))

    res = jnp.where(eye, 0.0, d * by_row * by_col)
    w_ref[...] = jnp.where(eye, by_row, 0.0) - half(res) * by_col

    def cond(carry):
        count, size = carry
        return (count < 12) & (size > 1e-7)

    def body(carry):
        count, _ = carry
        w = w_ref[...]
        s = dot6(dot6(w, d_ref[...]), w, 1)
        res = jnp.where(eye, s - 1.0, s)
        w_ref[...] = w - dot6(half(res), w)
        return count + 1, jnp.sum(res * res)

    _, size = lax.while_loop(cond, body, (jnp.int32(0), jnp.float32(1.0)))
    low_diag = jnp.min(jnp.where(eye, w_ref[...], 1.0))

    @pl.when(jnp.logical_not((size <= 1e-7) & (low_diag > 0.0)))
    def _():
        work_ref[:, :n] = d_ref[...]
        work_ref[:, n:] = jnp.where(eye, 1.0, 0.0)
        _, lane2 = iotas((n, 2 * n))
        row1, _ = iotas((n, 1))
        lane1 = lax.broadcasted_iota(jnp.int32, (1, 2 * n), 1)

        @pl.loop(0, n)
        def _(k):
            row = work_ref[pl.ds(k, 1), :]
            scale = lax.rsqrt(jnp.sum(jnp.where(lane1 == k, row, 0.0), axis=1, keepdims=True))
            row = row * scale
            full = work_ref[...]
            col = jnp.sum(jnp.where(lane2 == k, full, 0.0), axis=1, keepdims=True) * scale
            work_ref[...] = full - jnp.where(row1 > k, col, 0.0) * row
            work_ref[pl.ds(k, 1), :] = row

        w_ref[...] = work_ref[:, n:]


def pair(a, b):
    return a * (a + 1) // 2 + b


def chain_kernel(swap_ref, k_ref, out_ref, k_s, w_s, low_s, work_s):
    n = k_ref.shape[-1]
    for i in range(k_ref.shape[0]):
        k_s[i] = k_ref[i]
    for s in range(PANELS):
        invert_block(k_s.at[pair(s, s)], w_s.at[s], work_s)
        w = w_s[s]
        for k in range(s):
            out_ref[pair(s, k)] = dot6(w, low_s[pair(s, k)])
        h = n // 2

        @pl.when(swap_ref[0] == 0)
        def _():
            out_ref[pair(s, s)] = w

        @pl.when(swap_ref[0] != 0)
        def _():
            out_ref[pair(s, s), :, :h] = w[:, h:]
            out_ref[pair(s, s), :, h:] = w[:, :h]

        for a in range(s + 1, PANELS):
            low_s[pair(a, s)] = dot6(k_s[pair(a, s)], w, 1)
        for a in range(s + 1, PANELS):
            for b in range(s + 1, a + 1):
                k_s[pair(a, b)] = k_s[pair(a, b)] - dot6(low_s[pair(a, s)], low_s[pair(b, s)], 1)


def chain(swap, corner):
    count, n, _ = corner.shape
    return pl.pallas_call(
        chain_kernel,
        out_shape=jax.ShapeDtypeStruct(corner.shape, jnp.float32),
        in_specs=[pl.BlockSpec(memory_space=pltpu.SMEM), pl.BlockSpec(memory_space=pltpu.VMEM)],
        out_specs=pl.BlockSpec(memory_space=pltpu.VMEM),
        scratch_shapes=[pltpu.VMEM((count, n, n), jnp.float32), pltpu.VMEM((PANELS, n, n), jnp.float32),
                        pltpu.VMEM((count, n, n), jnp.float32), pltpu.VMEM((n, 2 * n), jnp.float32)],
        interpret=INTERPRET,
    )(swap, corner)


def spec(space=pltpu.VMEM):
    return pl.BlockSpec(memory_space=space)


def f32(*shape):
    return jax.ShapeDtypeStruct(shape, jnp.float32)


def bf16(*shape):
    return jax.ShapeDtypeStruct(shape, jnp.bfloat16)


def gather_kernel(rows, cols, info, trailing, corner_keep, corner_give, *refs):
    keeps, (gives, sem) = refs[:PANELS], refs[PANELS:]
    my_row, my_col, mine = info[PANELS], info[PANELS + 1], info[PANELS + 2]
    half = NB // 2
    blk_cols = trailing.shape[1] // NB

    def copy(row, col, out):
        source = trailing.at[
            pl.ds(pl.multiple_of(row, half), half), pl.ds(pl.multiple_of(col, NB), NB)
        ]
        return pltpu.make_async_copy(source, out, sem)

    plans = []
    for a in range(PANELS):
        for b in range(a + 1):
            n = pair(a, b)
            owner = (lax.rem(info[a], rows) == my_row) & (lax.rem(info[b], cols) == my_col)
            per = PANELS * (PANELS + 1) // 4
            place = (n // per == mine, n % per)
            row, col = lax.div(info[a], rows) * NB, lax.div(info[b], cols) * NB
            for keep in (True, False):
                out = corner_keep if keep else corner_give
                jobs = [(row + h * half, col, out.at[2 * place[1] + h]) for h in range(2)]
                plans.append((place[0] == keep, owner, jobs))
    for s in range(PANELS):
        owner = lax.rem(info[s], rows) == my_row
        row = lax.div(info[s], rows) * NB
        jobs = []
        for j in range(blk_cols):
            jobs.append((row + mine * half, j * NB, keeps[s].at[j]))
            jobs.append((row + (1 - mine) * half, j * NB, gives.at[s * blk_cols + j]))
        plans.append((True, owner, jobs))
    for there, owner, jobs in plans:

        @pl.when(there & owner)
        def _():
            for job in jobs:
                copy(*job).start()

        @pl.when(there & jnp.logical_not(owner))
        def _():
            for _, _, out in jobs:
                out[...] = jnp.zeros_like(out)

    for there, owner, jobs in plans:

        @pl.when(there & owner)
        def _():
            for job in jobs:
                copy(*job).wait()


def gather(info, trailing, rows, cols):
    half = NB // 2
    blk_cols = trailing.shape[1] // NB
    part = f32(PANELS * (PANELS + 1) // 2, half, NB)
    shapes = [part, part] + [f32(blk_cols, half, NB)] * PANELS
    shapes.append(f32(PANELS * blk_cols, half, NB))
    return pl.pallas_call(
        lambda *refs: gather_kernel(rows, cols, *refs),
        out_shape=shapes,
        in_specs=[spec(pltpu.SMEM), spec(pl.ANY)],
        out_specs=[spec()] * len(shapes),
        scratch_shapes=[pltpu.SemaphoreType.DMA],
        interpret=INTERPRET,
        cost_estimate=pl.CostEstimate(flops=0, bytes_accessed=16 << 20, transcendentals=0),
    )(info, trailing)


def halves(x):
    high = x.astype(jnp.bfloat16)
    return high, (x - high.astype(jnp.float32)).astype(jnp.bfloat16)


def is_used(info, block, step):
    used = False
    for k in range(step):
        used = used | (block == info[k])
    return used


def params():
    return pltpu.CompilerParams(vmem_limit_bytes=VMEM_LIMIT)


def cost(flops, mib):
    return pl.CostEstimate(flops=flops, bytes_accessed=mib << 20, transcendentals=0)


def block_of(name):
    return pl.BlockSpec((1, NB, NB), lambda i: (pair(*name), 0, 0))


def col_kernel(cols, info, *refs):
    raw, solved = refs[: 2 * PANELS - 2], refs[2 * PANELS - 2 : -3]
    parts, rest, left = refs[-3:]
    block = pl.program_id(0) * cols + info[PANELS + 1]
    last = PANELS - 1

    @pl.when(pl.program_id(0) == 0)
    def _():
        for n, ref in enumerate(solved):
            left[n] = left6(ref[0])

    facs = []
    for s in range(last):
        full = jnp.concatenate([raw[2 * s][0], raw[2 * s + 1][0]], axis=0)
        fac = bdot(left[pair(s, s)], right6(full))
        for k in range(s):
            fac = fac - bdot(left[pair(s, k)], facs[k])
        fac = jnp.where(is_used(info, block, s), 0.0, fac)
        facs.append(right6(fac))
        for i, part in enumerate(halves(fac)):
            at = (2 * s + i) * NB
            parts[0, at : at + NB] = part
    total = None
    for k in range(last):
        term = bdot(left[pair(last, k)], facs[k])
        total = term if total is None else total + term
    rest[0] = total


def col_factor(cols, info, raw, solved):
    count = raw[0].shape[0]
    last = PANELS - 1
    names = [(a, b) for a in range(PANELS) for b in range(a + 1)][:-1]
    part = pl.BlockSpec((1, NB // 2, NB), lambda i: (i, 0, 0))
    return pl.pallas_call(
        lambda *refs: col_kernel(cols, *refs),
        grid=(count,),
        out_shape=[bf16(count, 2 * last * NB, NB), f32(count, NB, NB)],
        in_specs=[spec(pltpu.SMEM)] + [part] * len(raw) + [block_of(n) for n in names],
        out_specs=[
            pl.BlockSpec((1, 2 * last * NB, NB), lambda i: (i, 0, 0)),
            pl.BlockSpec((1, NB, NB), lambda i: (i, 0, 0)),
        ],
        scratch_shapes=[pltpu.VMEM((len(names), NB, 6 * NB), jnp.bfloat16)],
        compiler_params=params(),
        interpret=INTERPRET,
        cost_estimate=cost(60 * count * NB**3, 12),
    )(info, *raw, *[solved] * len(names))


def fetch(info, sources, raw, sem):
    for which, source in enumerate(sources):

        @pl.when(info[PANELS + 3] == which)
        def _():
            copy = pltpu.make_async_copy(source, raw, sem)
            copy.start()
            copy.wait()


def row_kernel(s, rows, count, info, *refs):
    sources, refs = refs[:count], refs[count:]
    last = PANELS - 1
    total = (s + 1) + (PANELS - 1 if s == last - 1 else 0)
    solved, refs = refs[:total], refs[total:]
    before, refs = refs[:s], refs[s:]
    out, parts, raw, sem = refs[0], refs[1], refs[-2], refs[-1]
    step = pl.program_id(0)

    @pl.when(step == 0)
    def _():
        fetch(info, sources, raw, sem)

    full = jnp.concatenate([raw[0, step], raw[1, step]], axis=0)
    fac = dot6(full.T, solved[s][0], 1)
    facs = [ref[...] for ref in before]
    for k in range(s):
        fac = fac - dot6(facs[k], solved[k][0], 1)
    fac = jnp.where(is_used(info, step * rows + info[PANELS], s), 0.0, fac)
    out[...] = fac
    for i, part in enumerate(halves(fac)):
        parts[:, i * NB : (i + 1) * NB] = part
    if s == last - 1:
        facs.append(fac)
        rest = None
        for k in range(last):
            term = dot6(facs[k], solved[s + 1 + k][0], 1)
            rest = term if rest is None else rest + term
        refs[2][...] = rest


def row_factor(s, rows, info, sources, solved, before):
    raw = sources[0].shape
    count = raw[1]
    height = count * NB
    names = [(s, k) for k in range(s + 1)]
    shapes = [f32(height, PANELS * NB), bf16(height, 2 * NB)]
    specs = [
        pl.BlockSpec((NB, NB), lambda i: (i, s)),
        pl.BlockSpec((NB, 2 * NB), lambda i: (i, 0)),
    ]
    if s == PANELS - 2:
        names += [(PANELS - 1, k) for k in range(PANELS - 1)]
        shapes.append(f32(height, NB))
        specs.append(pl.BlockSpec((NB, NB), lambda i: (i, 0)))

    def column(k):
        return pl.BlockSpec((NB, NB), lambda i: (i, k))

    return pl.pallas_call(
        lambda *refs: row_kernel(s, rows, len(sources), *refs),
        grid=(count,),
        out_shape=shapes,
        in_specs=[spec(pltpu.SMEM)]
        + [spec(pl.ANY)] * len(sources)
        + [block_of(n) for n in names]
        + [column(k) for k in range(s)],
        out_specs=specs,
        scratch_shapes=[pltpu.VMEM(raw, jnp.float32), pltpu.SemaphoreType.DMA],
        input_output_aliases={1 + len(sources) + len(names): 0} if s else {},
        compiler_params=params(),
        interpret=INTERPRET,
        cost_estimate=cost(12 * len(names) * count * NB**3, 8),
    )(info, *sources, *[solved] * len(names), *before * s)


def own_kernel(ratio, info, half, other, out, sem):
    group = info[PANELS + 4]
    copies = []
    for h, part in enumerate((half, other)):
        for i in range(out.shape[1]):
            copies.append(
                pltpu.make_async_copy(part.at[i * ratio + group], out.at[h, i], sem)
            )
    for copy in copies:
        copy.start()
    for copy in copies:
        copy.wait()


def own_rows(ratio, info, half, other):
    return pl.pallas_call(
        lambda *refs: own_kernel(ratio, *refs),
        out_shape=f32(2, half.shape[0] // ratio, *half.shape[1:]),
        in_specs=[spec(pltpu.SMEM), spec(pl.ANY), spec(pl.ANY)],
        out_specs=spec(),
        scratch_shapes=[pltpu.SemaphoreType.DMA],
        interpret=INTERPRET,
        cost_estimate=pl.CostEstimate(flops=0, bytes_accessed=2 << 20, transcendentals=0),
    )(info, half, other)


def set_left(left, parts):
    for k, part in enumerate(parts):
        for i, at in enumerate((0, 1, 0)):
            to = (3 * k + i) * NB
            left[:, to : to + NB] = part[:, at * NB : (at + 1) * NB]


def early_kernel(info, current, cparts, *refs):
    rparts, out, left = refs[:-2], refs[-2], refs[-1]

    @pl.when(pl.program_id(0) == 0)
    def _():
        set_left(left, rparts)

    blocks = []
    for k in range(len(rparts)):
        high = cparts[0, 2 * k * NB : (2 * k + 1) * NB]
        low = cparts[0, (2 * k + 1) * NB : (2 * k + 2) * NB]
        blocks += [low, high, high]
    right = jnp.concatenate(blocks, axis=0)
    out[...] = current[...] - jnp.dot(left[...], right, preferred_element_type=jnp.float32)


def early_update(info, current, cparts, rparts):
    height, width = current.shape
    strip = pl.BlockSpec((height, NB), lambda i: (0, i))
    return pl.pallas_call(
        early_kernel,
        grid=(width // NB,),
        out_shape=f32(height, width),
        in_specs=[
            spec(pltpu.SMEM),
            strip,
            pl.BlockSpec((1,) + cparts.shape[1:], lambda i: (i, 0, 0)),
        ]
        + [spec()] * len(rparts),
        out_specs=strip,
        scratch_shapes=[pltpu.VMEM((height, 3 * len(rparts) * NB), jnp.bfloat16)],
        compiler_params=params(),
        interpret=INTERPRET,
        cost_estimate=cost(12 * height * width * NB, 24),
    )(info, current, cparts, *rparts)


def last_kernel(rows, cols, count, info, *refs):
    sources, refs = refs[:count], refs[count:]
    current, half, other, rest, w, row_rest, _, out, fout = refs[:9]
    raw, fac_s, parts, left, w6, sem, out_sem = refs[9:]
    last = PANELS - 1
    step = pl.program_id(0)
    blk_rows = raw.shape[1]
    write = pltpu.make_async_copy(fac_s, fout.at[:, pl.ds(last * NB, NB)], out_sem)

    @pl.when(step == 0)
    def _():
        fetch(info, sources, raw, sem)
        w6[...] = left6(w[0])
        for i in range(blk_rows):
            at = slice(i * NB, (i + 1) * NB)
            full = jnp.concatenate([raw[0, i], raw[1, i]], axis=0)
            fac = bdot(w6[...], right6(full)).T - row_rest[at]
            fac = jnp.where(is_used(info, i * rows + info[PANELS], last), 0.0, fac)
            fac_s[at] = fac
            high, low = halves(fac)
            parts[at, :NB] = high
            parts[at, NB:] = low
        set_left(left, [parts])

    @pl.when(step == 1)
    def _():
        write.start()

    block = step * cols + info[PANELS + 1]
    fac = bdot(w6[...], right6(jnp.concatenate([half[0], other[0]], axis=0))) - rest[0]
    high, low = halves(jnp.where(is_used(info, block, last), 0.0, fac))
    right = jnp.concatenate([low, high, high], axis=0)
    value = current[...] - jnp.dot(left[...], right, preferred_element_type=jnp.float32)
    dead = is_used(info, block, PANELS)
    for i in range(blk_rows):
        used = dead | is_used(info, i * rows + info[PANELS], PANELS)
        at = slice(i * NB, (i + 1) * NB)
        out[at, :] = jnp.where(used, 0.0, value[at])

    @pl.when(step == pl.num_programs(0) - 1)
    def _():
        write.wait()


def last_update(rows, cols, info, sources, current, raw, rest, solved, row_rest, out):
    height, width = current.shape
    strip = pl.BlockSpec((height, NB), lambda i: (0, i))
    part = pl.BlockSpec((1, NB // 2, NB), lambda i: (i, 0, 0))
    last = PANELS - 1
    count = len(sources)
    return pl.pallas_call(
        lambda *refs: last_kernel(rows, cols, count, *refs),
        grid=(width // NB,),
        out_shape=[f32(height, width), f32(*out.shape)],
        in_specs=[spec(pltpu.SMEM)]
        + [spec(pl.ANY)] * count
        + [strip, part, part, pl.BlockSpec((1, NB, NB), lambda i: (i, 0, 0))]
        + [block_of((last, last)), spec(), spec(pl.ANY)],
        out_specs=[strip, spec(pl.ANY)],
        scratch_shapes=[
            pltpu.VMEM(sources[0].shape, jnp.float32),
            pltpu.VMEM((height, NB), jnp.float32),
            pltpu.VMEM((height, 2 * NB), jnp.bfloat16),
            pltpu.VMEM((height, 3 * NB), jnp.bfloat16),
            pltpu.VMEM((NB, 6 * NB), jnp.bfloat16),
            pltpu.SemaphoreType.DMA,
            pltpu.SemaphoreType.DMA,
        ],
        input_output_aliases={count + 7: 1},
        compiler_params=params(),
        interpret=INTERPRET,
        cost_estimate=cost(6 * height * width * NB, 24),
    )(info, *sources, current, *raw, rest, solved, row_rest, out)


class Net:
    def __init__(self, rows, cols):
        self.rows, self.cols = rows, cols
        self.row_bits = [1 << i for i in range(1, rows.bit_length() - 1)]
        self.col_bits = [1 << i for i in range(cols.bit_length() - 1)]

    def send(self, value, target):
        pairs = []
        for r in range(self.rows):
            for c in range(self.cols):
                to = target(r, c)
                if to is not None:
                    pairs.append((r * self.cols + c, to[0] * self.cols + to[1]))
        return lax.ppermute(value, AXES, pairs)

    def core(self, value):
        return self.send(value, lambda r, c: (r ^ 1, c))

    def step_bit(self, step, core):
        return self.row_bits[(step + core) % len(self.row_bits)]

    def row_step(self, value, step, turn=0):
        return self.send(value, lambda r, c: (r ^ self.step_bit(step, (r + turn) & 1), c))

    def col_step(self, value, bit):
        return self.send(value, lambda r, c: (r, c ^ bit))

    def my_bit(self, my_row, mine, step, turn):
        even = (my_row & self.step_bit(step, turn)) != 0
        odd = (my_row & self.step_bit(step, 1 - turn)) != 0
        return jnp.where(mine == 0, even, odd).astype(jnp.int32)


def pick(value, index):
    return lax.dynamic_index_in_dim(value, index, 0, keepdims=False)


def spread_corner(net, part, my_row, mine):
    tail = part.shape[1:]
    bits = []
    turn = 0
    for step in range(len(net.row_bits)):
        bit = net.my_bit(my_row, mine, step, turn)
        bits.append(bit)
        part = part.reshape((2, -1) + tail)
        part = pick(part, bit) + net.row_step(pick(part, 1 - bit), step, turn)
    for bit in net.col_bits:
        part = part + net.col_step(part, bit)
    for step in reversed(range(len(net.row_bits))):
        other = net.row_step(part, step, turn)
        low = bits[step] == 0
        part = jnp.concatenate([jnp.where(low, part, other), jnp.where(low, other, part)])
    other = net.core(part)
    low = mine == 0
    return jnp.concatenate([jnp.where(low, part, other), jnp.where(low, other, part)])


def spread_rows(net, source, is_source, direct):
    if (net.rows, net.cols) != (8, 4):
        value = jnp.where(is_source, source, 0.0)
        for bit in net.col_bits:
            value = value + net.col_step(value, bit)
        return [value]

    def hop(first, second):
        def target(r, c):
            up = (r // 2) % 2 == 0
            line = c if up else 3 - c
            near = (r % 2 == 0) == up
            to = (first if near else second).get(line)
            if to is None:
                return None
            return (r, to if up else 3 - to)

        return target

    got1 = net.send(source, hop({0: 1}, {1: 2}))
    if direct:
        got2 = net.send(source, hop({0: 2}, {1: 3}))
        got3 = net.send(source, hop({0: 3}, {1: 0}))
        return [source, got1, got2, got3]
    got2 = net.send(got1, hop({1: 2}, {2: 3}))
    third = jnp.where(is_source, source, got2)
    got3 = net.send(third, hop({2: 3}, {1: 0}))
    return [source, got1, got2, got3]


def source_code(net, my_row, my_col):
    if (net.rows, net.cols) != (8, 4):
        return jnp.int32(0)
    up = (my_row & 2) == 0
    line = jnp.where(up, my_col, 3 - my_col)
    near = ((my_row & 1) == 0) == up
    return jnp.where(near, line, (line + 3) & 3)


def run(panel, trailing):
    rows = lax.axis_size("row")
    cols = lax.axis_size("col")
    my_row = lax.axis_index("row")
    my_col = lax.axis_index("col")
    net = Net(rows, cols)
    mine = my_row & 1
    _, loc_cols = trailing.shape
    blk_cols = loc_cols // NB
    ratio = rows // cols
    half = NB // 2
    group = lax.div(my_row, cols)
    code = source_code(net, my_row, my_col)
    extra = jnp.stack([my_row, my_col, mine, code, group])
    info = jnp.concatenate([panel[:PANELS], extra])
    is_source = my_col == lax.rem(my_row, cols)

    corner, corner_give, *keeps, gives = gather(info, trailing, rows, cols)
    got = net.core(gives).reshape(PANELS, blk_cols, half, NB)
    corner = corner + net.core(corner_give)
    corner = spread_corner(net, corner.reshape(rows, -1, NB), my_row, mine)
    solved = chain(info[PANELS + 2 : PANELS + 3], corner.reshape(-1, NB, NB))

    parts, sources = [], []
    for s in range(PANELS):
        part = keeps[s] + got[s]
        for step in range(len(net.row_bits)):
            part = part + net.row_step(part, step)
        parts.append((part, net.core(part)))
        own = own_rows(ratio, info, *parts[s])
        sources.append(spread_rows(net, own, is_source, s == PANELS - 1))
    cparts, col_rest = col_factor(cols, info, [v for p in parts[:-1] for v in p], solved)
    out, rparts = (), []
    for s in range(PANELS - 1):
        out, *got = row_factor(s, rows, info, sources[s], solved, [out])
        rparts.append(got[0])
    current = early_update(info, trailing, cparts, rparts)
    current, out = last_update(
        rows, cols, info, sources[-1], current, parts[-1], col_rest, solved, got[1], out
    )
    return (out, current)


def solution(mesh):
    in_specs = (P(), P("row", "col"))
    out_specs = (P("row", None), P("row", "col"))
    return jax.shard_map(run, mesh=mesh, in_specs=in_specs, out_specs=out_specs, check_vma=False)
```

```python
import jax
import jax.numpy as jnp
from jax import lax
from jax.experimental import pallas as pl
from jax.experimental.pallas import tpu as pltpu
from jax.sharding import PartitionSpec as P


NB = 256
PANELS = 3
AXES = ("row", "col")
INTERPRET = False
VMEM_LIMIT = 24 << 20


def thirds(x):
    high = x.astype(jnp.bfloat16)
    rest = x - high.astype(jnp.float32)
    mid = rest.astype(jnp.bfloat16)
    return high, mid, (rest - mid.astype(jnp.float32)).astype(jnp.bfloat16)


def left6(a):
    high, mid, low = thirds(a)
    return jnp.concatenate([mid, low, high, mid, high, high], axis=1)


def right6(b, axis=0):
    high, mid, low = thirds(b)
    return jnp.concatenate([mid, high, low, high, mid, high], axis=axis)


def bdot(left, right, axis=0):
    return lax.dot_general(
        left, right, (((1,), (axis,)), ((), ())), preferred_element_type=jnp.float32
    )


def dot6(a, b, axis=0):
    return bdot(left6(a), right6(b, axis), axis)


def iotas(shape):
    return (lax.broadcasted_iota(jnp.int32, shape, 0), lax.broadcasted_iota(jnp.int32, shape, 1))


def invert_block(d_ref, w_ref, work_ref):
    n = d_ref.shape[0]
    ii, jj = iotas((n, n))
    eye = ii == jj
    d = d_ref[...]
    diag = jnp.where(eye, d, 0.0)
    by_col = lax.rsqrt(jnp.sum(diag, axis=0, keepdims=True))
    by_row = lax.rsqrt(jnp.sum(diag, axis=1, keepdims=True))

    def half(r):
        return jnp.where(ii > jj, r, jnp.where(eye, 0.5 * r, 0.0))

    res = jnp.where(eye, 0.0, d * by_row * by_col)
    w_ref[...] = jnp.where(eye, by_row, 0.0) - half(res) * by_col

    def cond(carry):
        count, size = carry
        return (count < 12) & (size > 1e-7)

    def body(carry):
        count, _ = carry
        w = w_ref[...]
        s = dot6(dot6(w, d_ref[...]), w, 1)
        res = jnp.where(eye, s - 1.0, s)
        w_ref[...] = w - dot6(half(res), w)
        return count + 1, jnp.sum(res * res)

    _, size = lax.while_loop(cond, body, (jnp.int32(0), jnp.float32(1.0)))
    low_diag = jnp.min(jnp.where(eye, w_ref[...], 1.0))

    @pl.when(jnp.logical_not((size <= 1e-7) & (low_diag > 0.0)))
    def _():
        work_ref[:, :n] = d_ref[...]
        work_ref[:, n:] = jnp.where(eye, 1.0, 0.0)
        _, lane2 = iotas((n, 2 * n))
        row1, _ = iotas((n, 1))
        lane1 = lax.broadcasted_iota(jnp.int32, (1, 2 * n), 1)

        @pl.loop(0, n)
        def _(k):
            row = work_ref[pl.ds(k, 1), :]
            scale = lax.rsqrt(jnp.sum(jnp.where(lane1 == k, row, 0.0), axis=1, keepdims=True))
            row = row * scale
            full = work_ref[...]
            col = jnp.sum(jnp.where(lane2 == k, full, 0.0), axis=1, keepdims=True) * scale
            work_ref[...] = full - jnp.where(row1 > k, col, 0.0) * row
            work_ref[pl.ds(k, 1), :] = row

        w_ref[...] = work_ref[:, n:]


def pair(a, b):
    return a * (a + 1) // 2 + b


def chain_kernel(k_ref, out_ref, k_s, w_s, low_s, work_s):
    for i in range(k_ref.shape[0]):
        k_s[i] = k_ref[i]
    for s in range(PANELS):
        invert_block(k_s.at[pair(s, s)], w_s.at[s], work_s)
        w = w_s[s]
        for k in range(s):
            out_ref[pair(s, k)] = dot6(w, low_s[pair(s, k)])
        out_ref[pair(s, s)] = w
        for a in range(s + 1, PANELS):
            low_s[pair(a, s)] = dot6(k_s[pair(a, s)], w, 1)
        for a in range(s + 1, PANELS):
            for b in range(s + 1, a + 1):
                k_s[pair(a, b)] = k_s[pair(a, b)] - dot6(low_s[pair(a, s)], low_s[pair(b, s)], 1)


def chain(corner):
    count, n, _ = corner.shape
    return pl.pallas_call(
        chain_kernel,
        out_shape=jax.ShapeDtypeStruct(corner.shape, jnp.float32),
        in_specs=[pl.BlockSpec(memory_space=pltpu.VMEM)],
        out_specs=pl.BlockSpec(memory_space=pltpu.VMEM),
        scratch_shapes=[pltpu.VMEM((count, n, n), jnp.float32), pltpu.VMEM((PANELS, n, n), jnp.float32),
                        pltpu.VMEM((count, n, n), jnp.float32), pltpu.VMEM((n, 2 * n), jnp.float32)],
        interpret=INTERPRET,
    )(corner)


def spec(space=pltpu.VMEM):
    return pl.BlockSpec(memory_space=space)


def f32(*shape):
    return jax.ShapeDtypeStruct(shape, jnp.float32)


def bf16(*shape):
    return jax.ShapeDtypeStruct(shape, jnp.bfloat16)


def gather_kernel(rows, cols, info, trailing, corner_keep, corner_give, *refs):
    keeps, (gives, sem) = refs[:PANELS], refs[PANELS:]
    my_row, my_col, mine = info[PANELS], info[PANELS + 1], info[PANELS + 2]
    half = NB // 2
    count = trailing.shape[1] // NB // 2
    stream = info[PANELS + 4]

    def copy(row, col, out):
        source = trailing.at[
            pl.ds(pl.multiple_of(row, half), out.shape[0]), pl.ds(pl.multiple_of(col, NB), NB)
        ]
        return pltpu.make_async_copy(source, out, sem)

    plans = []
    for a in range(PANELS):
        for b in range(a + 1):
            n = pair(a, b)
            owner = (lax.rem(info[a], rows) == my_row) & (lax.rem(info[b], cols) == my_col)
            per = PANELS * (PANELS + 1) // 4
            place = (n // per == mine, n % per)
            row, col = lax.div(info[a], rows) * NB, lax.div(info[b], cols) * NB
            for keep in (True, False):
                out = corner_keep if keep else corner_give
                jobs = [(row + h * half, col, out.at[2 * place[1] + h]) for h in range(2)]
                plans.append((place[0] == keep, owner, jobs))
    for s in range(PANELS):
        owner = lax.rem(info[s], rows) == my_row
        row = lax.div(info[s], rows) * NB
        jobs = []
        for j in range(count):
            jobs.append((row, (2 * j + stream) * NB, keeps[s].at[j]))
            jobs.append((row, (2 * j + 1 - stream) * NB, gives.at[s * count + j]))
        plans.append((True, owner, jobs))
    for there, owner, jobs in plans:

        @pl.when(there & owner)
        def _():
            for job in jobs:
                copy(*job).start()

        @pl.when(there & jnp.logical_not(owner))
        def _():
            for _, _, out in jobs:
                out[...] = jnp.zeros_like(out)

    for there, owner, jobs in plans:

        @pl.when(there & owner)
        def _():
            for job in jobs:
                copy(*job).wait()


def gather(info, trailing, rows, cols):
    count = trailing.shape[1] // NB // 2
    part = f32(PANELS * (PANELS + 1) // 2, NB // 2, NB)
    shapes = [part, part] + [f32(count, NB, NB)] * PANELS
    shapes.append(f32(PANELS * count, NB, NB))
    return pl.pallas_call(
        lambda *refs: gather_kernel(rows, cols, *refs),
        out_shape=shapes,
        in_specs=[spec(pltpu.SMEM), spec(pl.ANY)],
        out_specs=[spec()] * len(shapes),
        scratch_shapes=[pltpu.SemaphoreType.DMA],
        interpret=INTERPRET,
        cost_estimate=pl.CostEstimate(flops=0, bytes_accessed=16 << 20, transcendentals=0),
    )(info, trailing)


def halves(x):
    high = x.astype(jnp.bfloat16)
    return high, (x - high.astype(jnp.float32)).astype(jnp.bfloat16)


def is_used(info, block, step):
    used = False
    for k in range(step):
        used = used | (block == info[k])
    return used


def params():
    return pltpu.CompilerParams(vmem_limit_bytes=VMEM_LIMIT)


def cost(flops, mib):
    return pl.CostEstimate(flops=flops, bytes_accessed=mib << 20, transcendentals=0)


def block_of(name):
    return pl.BlockSpec((1, NB, NB), lambda i: (pair(*name), 0, 0))


def col_kernel(first, cols, info, *refs):
    width = (PANELS - 1 if first == 0 else PANELS) - first
    raw, refs = refs[:width], refs[width:]
    solved, refs = (refs[:-3], refs[-3:]) if first == 0 else (refs[:1], refs[1:])
    block = (2 * pl.program_id(0) + info[PANELS + 4]) * cols + info[PANELS + 1]
    if first:
        rest, out = refs
        fac = dot6(solved[0][0], raw[0][0]) - rest[0]
        out[0, 0] = jnp.where(is_used(info, block, first), 0.0, fac)
        return
    out, rest, left = refs

    @pl.when(pl.program_id(0) == 0)
    def _():
        for n, ref in enumerate(solved):
            left[n] = left6(ref[0])

    facs = []
    for s in range(width):
        fac = bdot(left[pair(s, s)], right6(raw[s][0]))
        for k in range(s):
            fac = fac - bdot(left[pair(s, k)], facs[k])
        fac = jnp.where(is_used(info, block, s), 0.0, fac)
        facs.append(right6(fac))
        out[s, 0] = fac
    total = None
    for k in range(width):
        term = bdot(left[pair(width, k)], facs[k])
        total = term if total is None else total + term
    rest[0] = total


def col_factor(first, cols, info, raw, solved, rest):
    count = raw[0].shape[0]
    width = len(raw)
    one = pl.BlockSpec((1, NB, NB), lambda i: (i, 0, 0))
    outs = [f32(width, count, NB, NB)]
    specs = [pl.BlockSpec((width, 1, NB, NB), lambda i: (0, i, 0, 0))]
    scratch = []
    if first:
        names = [(first, first)]
    else:
        names = [(a, b) for a in range(PANELS) for b in range(a + 1)][:-1]
        outs.append(f32(count, NB, NB))
        specs.append(one)
        scratch.append(pltpu.VMEM((len(names), NB, 6 * NB), jnp.bfloat16))
    return pl.pallas_call(
        lambda *refs: col_kernel(first, cols, *refs),
        grid=(count,),
        out_shape=outs,
        in_specs=[spec(pltpu.SMEM)]
        + [one] * width
        + [block_of(n) for n in names]
        + [one] * len(rest),
        out_specs=specs,
        scratch_shapes=scratch,
        compiler_params=params(),
        interpret=INTERPRET,
        cost_estimate=cost(12 * len(names) * count * NB**3, 8),
    )(info, *raw, *[solved] * len(names), *rest)


def fetch(info, sources, raw, sem):
    for which, source in enumerate(sources):

        @pl.when(info[PANELS + 3] == which)
        def _():
            copy = pltpu.make_async_copy(source, raw, sem)
            copy.start()
            copy.wait()


def row_kernel(s, rows, count, info, *refs):
    sources, refs = refs[:count], refs[count:]
    last = PANELS - 1
    total = (s + 1) + (PANELS - 1 if s == last - 1 else 0)
    solved, refs = refs[:total], refs[total:]
    before, refs = refs[:s], refs[s:]
    out, parts, raw, sem = refs[0], refs[1], refs[-2], refs[-1]
    step = pl.program_id(0)

    @pl.when(step == 0)
    def _():
        fetch(info, sources, raw, sem)

    fac = dot6(raw[step].T, solved[s][0], 1)
    facs = [ref[...] for ref in before]
    for k in range(s):
        fac = fac - dot6(facs[k], solved[k][0], 1)
    fac = jnp.where(is_used(info, step * rows + info[PANELS], s), 0.0, fac)
    out[...] = fac
    for i, part in enumerate(halves(fac)):
        parts[:, i * NB : (i + 1) * NB] = part
    if s == last - 1:
        facs.append(fac)
        rest = None
        for k in range(last):
            term = dot6(facs[k], solved[s + 1 + k][0], 1)
            rest = term if rest is None else rest + term
        refs[2][...] = rest


def row_factor(s, rows, info, sources, solved, before):
    raw = sources[0].shape
    count = raw[0]
    height = count * NB
    names = [(s, k) for k in range(s + 1)]
    shapes = [f32(height, PANELS * NB), bf16(height, 2 * NB)]
    specs = [
        pl.BlockSpec((NB, NB), lambda i: (i, s)),
        pl.BlockSpec((NB, 2 * NB), lambda i: (i, 0)),
    ]
    if s == PANELS - 2:
        names += [(PANELS - 1, k) for k in range(PANELS - 1)]
        shapes.append(f32(height, NB))
        specs.append(pl.BlockSpec((NB, NB), lambda i: (i, 0)))

    def column(k):
        return pl.BlockSpec((NB, NB), lambda i: (i, k))

    return pl.pallas_call(
        lambda *refs: row_kernel(s, rows, len(sources), *refs),
        grid=(count,),
        out_shape=shapes,
        in_specs=[spec(pltpu.SMEM)]
        + [spec(pl.ANY)] * len(sources)
        + [block_of(n) for n in names]
        + [column(k) for k in range(s)],
        out_specs=specs,
        scratch_shapes=[pltpu.VMEM(raw, jnp.float32), pltpu.SemaphoreType.DMA],
        input_output_aliases={1 + len(sources) + len(names): 0} if s else {},
        compiler_params=params(),
        interpret=INTERPRET,
        cost_estimate=cost(12 * len(names) * count * NB**3, 8),
    )(info, *sources, *[solved] * len(names), *before * s)


def set_left(left, parts):
    for k, part in enumerate(parts):
        for i, at in enumerate((0, 1, 0)):
            to = (3 * k + i) * NB
            left[:, to : to + NB] = part[:, at * NB : (at + 1) * NB]


def set_right(right, own, other):
    count = pl.num_programs(0) // 2
    step = pl.program_id(0)
    for there, fac in ((step < count, own), (step >= count, other)):

        @pl.when(there)
        def _():
            for k in range(fac.shape[0]):
                high, low = halves(fac[k, 0])
                for i, part in enumerate((low, high, high)):
                    to = (3 * k + i) * NB
                    right[to : to + NB] = part


def column_at(count, step, info):
    stream = info[PANELS + 4]
    mine = step < count
    return 2 * jnp.where(mine, step, step - count) + jnp.where(mine, stream, 1 - stream)


def update_specs(height, width, panels):
    count = width // NB // 2
    strip = pl.BlockSpec((height, NB), lambda i, info: (0, column_at(count, i, info)))
    shape = (panels, 1, NB, NB)
    own = pl.BlockSpec(shape, lambda i, info: (0, jnp.minimum(i, count - 1), 0, 0))
    other = pl.BlockSpec(shape, lambda i, info: (0, jnp.maximum(i - count, 0), 0, 0))
    return strip, own, other


def early_kernel(info, current, own, other, *refs):
    rparts, out, left, right = refs[:-3], *refs[-3:]

    @pl.when(pl.program_id(0) == 0)
    def _():
        set_left(left, rparts)

    set_right(right, own, other)
    product = jnp.dot(left[...], right[...], preferred_element_type=jnp.float32)
    out[...] = current[...] - product


def early_update(info, current, own, other, rparts):
    height, width = current.shape
    panels = len(rparts)
    strip, mine, theirs = update_specs(height, width, panels)
    return pl.pallas_call(
        early_kernel,
        grid_spec=pltpu.PrefetchScalarGridSpec(
            num_scalar_prefetch=1,
            grid=(width // NB,),
            in_specs=[strip, mine, theirs] + [spec()] * panels,
            out_specs=strip,
            scratch_shapes=[
                pltpu.VMEM((height, 3 * panels * NB), jnp.bfloat16),
                pltpu.VMEM((3 * panels * NB, NB), jnp.bfloat16),
            ],
        ),
        out_shape=f32(height, width),
        compiler_params=params(),
        interpret=INTERPRET,
        cost_estimate=cost(12 * height * width * NB, 24),
    )(info, current, own, other, *rparts)


def last_kernel(rows, cols, count, info, *refs):
    sources, refs = refs[:count], refs[count:]
    current, own, other, w, row_rest, _, out, fout = refs[:8]
    raw, fac_s, left, right, sem, out_sem = refs[8:]
    last = PANELS - 1
    step = pl.program_id(0)
    blk_rows = raw.shape[0]
    write = pltpu.make_async_copy(fac_s, fout.at[:, pl.ds(last * NB, NB)], out_sem)

    @pl.when(step == 0)
    def _():
        fetch(info, sources, raw, sem)
        split = right6(w[0], 1)
        for i in range(blk_rows):
            at = slice(i * NB, (i + 1) * NB)
            fac = bdot(left6(raw[i].T), split, 1) - row_rest[at]
            fac = jnp.where(is_used(info, i * rows + info[PANELS], last), 0.0, fac)
            fac_s[at] = fac
            high, low = halves(fac)
            for k, part in enumerate((high, low, high)):
                left[at, k * NB : (k + 1) * NB] = part

    @pl.when(step == 1)
    def _():
        write.start()

    set_right(right, own, other)
    product = jnp.dot(left[...], right[...], preferred_element_type=jnp.float32)
    value = current[...] - product
    block = column_at(pl.num_programs(0) // 2, step, info) * cols + info[PANELS + 1]
    dead = is_used(info, block, PANELS)
    for i in range(blk_rows):
        used = dead | is_used(info, i * rows + info[PANELS], PANELS)
        at = slice(i * NB, (i + 1) * NB)
        out[at, :] = jnp.where(used, 0.0, value[at])

    @pl.when(step == pl.num_programs(0) - 1)
    def _():
        write.wait()


def last_update(rows, cols, info, sources, current, own, other, solved, row_rest, out):
    height, width = current.shape
    strip, mine, theirs = update_specs(height, width, 1)
    last = PANELS - 1
    count = len(sources)
    w = pl.BlockSpec((1, NB, NB), lambda i, info: (pair(last, last), 0, 0))
    return pl.pallas_call(
        lambda *refs: last_kernel(rows, cols, count, *refs),
        grid_spec=pltpu.PrefetchScalarGridSpec(
            num_scalar_prefetch=1,
            grid=(width // NB,),
            in_specs=[spec(pl.ANY)] * count
            + [strip, mine, theirs, w, spec(), spec(pl.ANY)],
            out_specs=[strip, spec(pl.ANY)],
            scratch_shapes=[
                pltpu.VMEM(sources[0].shape, jnp.float32),
                pltpu.VMEM((height, NB), jnp.float32),
                pltpu.VMEM((height, 3 * NB), jnp.bfloat16),
                pltpu.VMEM((3 * NB, NB), jnp.bfloat16),
                pltpu.SemaphoreType.DMA,
                pltpu.SemaphoreType.DMA,
            ],
        ),
        out_shape=[f32(height, width), f32(*out.shape)],
        input_output_aliases={count + 6: 1},
        compiler_params=params(),
        interpret=INTERPRET,
        cost_estimate=cost(6 * height * width * NB, 24),
    )(info, *sources, current, own, other, solved, row_rest, out)


class Net:
    def __init__(self, rows, cols):
        self.rows, self.cols = rows, cols
        self.row_bits = [1 << i for i in range(1, rows.bit_length() - 1)]
        self.col_bits = [1 << i for i in range(cols.bit_length() - 1)]

    def send(self, value, target):
        pairs = []
        for r in range(self.rows):
            for c in range(self.cols):
                to = target(r, c)
                if to is not None:
                    pairs.append((r * self.cols + c, to[0] * self.cols + to[1]))
        return lax.ppermute(value, AXES, pairs)

    def core(self, value):
        return self.send(value, lambda r, c: (r ^ 1, c))

    def step_bit(self, step, core):
        return self.row_bits[(step + core) % len(self.row_bits)]

    def row_step(self, value, step, turn=0):
        return self.send(value, lambda r, c: (r ^ self.step_bit(step, (r + turn) & 1), c))

    def stream(self, r, c):
        return (r + c + r // self.cols) & 1

    def raw_step(self, value, step):
        def target(r, c):
            g = self.stream(r, c)
            to = r ^ self.step_bit(step, g)
            return (to if self.stream(to, c) == g else to ^ 1, c)

        return self.send(value, target)

    def col_step(self, value, bit):
        return self.send(value, lambda r, c: (r, c ^ bit))

    def my_bit(self, my_row, mine, step, turn):
        even = (my_row & self.step_bit(step, turn)) != 0
        odd = (my_row & self.step_bit(step, 1 - turn)) != 0
        return jnp.where(mine == 0, even, odd).astype(jnp.int32)


def pick(value, index):
    return lax.dynamic_index_in_dim(value, index, 0, keepdims=False)


def spread_corner(net, part, my_row, mine):
    tail = part.shape[1:]
    bits = []
    turn = 0
    for step in range(len(net.row_bits)):
        bit = net.my_bit(my_row, mine, step, turn)
        bits.append(bit)
        part = part.reshape((2, -1) + tail)
        part = pick(part, bit) + net.row_step(pick(part, 1 - bit), step, turn)
    for bit in net.col_bits:
        part = part + net.col_step(part, bit)
    for step in reversed(range(len(net.row_bits))):
        other = net.row_step(part, step, turn)
        low = bits[step] == 0
        part = jnp.concatenate([jnp.where(low, part, other), jnp.where(low, other, part)])
    other = net.core(part)
    low = mine == 0
    return jnp.concatenate([jnp.where(low, part, other), jnp.where(low, other, part)])


def spread_rows(net, source, is_source, direct):
    if (net.rows, net.cols) != (8, 4):
        value = jnp.where(is_source, source, 0.0)
        for bit in net.col_bits:
            value = value + net.col_step(value, bit)
        return [value]

    def hop(first, second):
        def target(r, c):
            up = (r // 2) % 2 == 0
            line = c if up else 3 - c
            near = (r % 2 == 0) == up
            to = (first if near else second).get(line)
            if to is None:
                return None
            return (r, to if up else 3 - to)

        return target

    got1 = net.send(source, hop({0: 1}, {1: 2}))
    if direct:
        got2 = net.send(source, hop({0: 2}, {1: 3}))
        got3 = net.send(source, hop({0: 3}, {1: 0}))
        return [source, got1, got2, got3]
    got2 = net.send(got1, hop({1: 2}, {2: 3}))
    third = jnp.where(is_source, source, got2)
    got3 = net.send(third, hop({2: 3}, {1: 0}))
    return [source, got1, got2, got3]


def source_code(net, my_row, my_col):
    if (net.rows, net.cols) != (8, 4):
        return jnp.int32(0)
    up = (my_row & 2) == 0
    line = jnp.where(up, my_col, 3 - my_col)
    near = ((my_row & 1) == 0) == up
    return jnp.where(near, line, (line + 3) & 3)


def run(panel, trailing):
    rows = lax.axis_size("row")
    cols = lax.axis_size("col")
    my_row = lax.axis_index("row")
    my_col = lax.axis_index("col")
    net = Net(rows, cols)
    mine = my_row & 1
    loc_cols = trailing.shape[1]
    count = loc_cols // NB // 2
    ratio = rows // cols
    group = lax.div(my_row, cols)
    stream = (my_row + my_col + group) & 1
    code = source_code(net, my_row, my_col)
    extra = jnp.stack([my_row, my_col, mine, code, stream])
    info = jnp.concatenate([panel[:PANELS], extra])
    is_source = my_col == lax.rem(my_row, cols)

    corner, corner_give, *keeps, gives = gather(info, trailing, rows, cols)
    got = net.core(gives).reshape(PANELS, count, NB, NB)
    corner = corner + net.core(corner_give)
    corner = spread_corner(net, corner.reshape(rows, -1, NB), my_row, mine)
    solved = chain(corner.reshape(-1, NB, NB))

    raws, sources = [], []
    for s in range(PANELS):
        raw = keeps[s] + got[s]
        for step in range(len(net.row_bits)):
            raw = raw + net.raw_step(raw, step)
        raws.append(raw)
        own = raw
        if ratio != 2:
            other = net.core(raw)
            even = jnp.where(stream == 0, raw, other)
            odd = jnp.where(stream == 0, other, raw)
            own = jnp.stack([even, odd], axis=1).reshape(-1, ratio, NB, NB)
            own = lax.dynamic_index_in_dim(own, group, 1, keepdims=False)
        sources.append(spread_rows(net, own, is_source, s == PANELS - 1))
    last = PANELS - 1
    early, col_rest = col_factor(0, cols, info, raws[:last], solved, [])
    early_other = net.core(early)
    (late,) = col_factor(last, cols, info, raws[last:], solved, [col_rest])
    late_other = net.core(late)
    out, rparts = (), []
    for s in range(last):
        out, *got = row_factor(s, rows, info, sources[s], solved, [out])
        rparts.append(got[0])
    current = early_update(info, trailing, early, early_other, rparts)
    current, out = last_update(
        rows, cols, info, sources[last], current, late, late_other, solved, got[1], out
    )
    return (out, current)


def solution(mesh):
    in_specs = (P(), P("row", "col"))
    out_specs = (P("row", None), P("row", "col"))
    return jax.shard_map(run, mesh=mesh, in_specs=in_specs, out_specs=out_specs, check_vma=False)
```

```python
import jax
import jax.numpy as jnp
from jax import lax
from jax.experimental import pallas as pl
from jax.experimental.pallas import tpu as pltpu
from jax.sharding import PartitionSpec as P


NB = 256
PANELS = 3
AXES = ("row", "col")
INTERPRET = False
VMEM_LIMIT = 24 << 20


def thirds(x):
    high = x.astype(jnp.bfloat16)
    rest = x - high.astype(jnp.float32)
    mid = rest.astype(jnp.bfloat16)
    return high, mid, (rest - mid.astype(jnp.float32)).astype(jnp.bfloat16)


def left6(a):
    high, mid, low = thirds(a)
    return jnp.concatenate([mid, low, high, mid, high, high], axis=1)


def right6(b, axis=0):
    high, mid, low = thirds(b)
    return jnp.concatenate([mid, high, low, high, mid, high], axis=axis)


def bdot(left, right, axis=0):
    return lax.dot_general(
        left, right, (((1,), (axis,)), ((), ())), preferred_element_type=jnp.float32
    )


def dot6(a, b, axis=0):
    return bdot(left6(a), right6(b, axis), axis)


def iotas(shape):
    return (lax.broadcasted_iota(jnp.int32, shape, 0), lax.broadcasted_iota(jnp.int32, shape, 1))


def invert_block(d_ref, w_ref, work_ref):
    n = d_ref.shape[0]
    ii, jj = iotas((n, n))
    eye = ii == jj
    d = d_ref[...]
    diag = jnp.where(eye, d, 0.0)
    by_col = lax.rsqrt(jnp.sum(diag, axis=0, keepdims=True))
    by_row = lax.rsqrt(jnp.sum(diag, axis=1, keepdims=True))

    def half(r):
        return jnp.where(ii > jj, r, jnp.where(eye, 0.5 * r, 0.0))

    res = jnp.where(eye, 0.0, d * by_row * by_col)
    w_ref[...] = jnp.where(eye, by_row, 0.0) - half(res) * by_col

    def cond(carry):
        count, size = carry
        return (count < 12) & (size > 1e-7)

    def body(carry):
        count, _ = carry
        w = w_ref[...]
        s = dot6(dot6(w, d_ref[...]), w, 1)
        res = jnp.where(eye, s - 1.0, s)
        w_ref[...] = w - dot6(half(res), w)
        return count + 1, jnp.sum(res * res)

    _, size = lax.while_loop(cond, body, (jnp.int32(0), jnp.float32(1.0)))
    low_diag = jnp.min(jnp.where(eye, w_ref[...], 1.0))

    @pl.when(jnp.logical_not((size <= 1e-7) & (low_diag > 0.0)))
    def _():
        work_ref[:, :n] = d_ref[...]
        work_ref[:, n:] = jnp.where(eye, 1.0, 0.0)
        _, lane2 = iotas((n, 2 * n))
        row1, _ = iotas((n, 1))
        lane1 = lax.broadcasted_iota(jnp.int32, (1, 2 * n), 1)

        @pl.loop(0, n)
        def _(k):
            row = work_ref[pl.ds(k, 1), :]
            scale = lax.rsqrt(jnp.sum(jnp.where(lane1 == k, row, 0.0), axis=1, keepdims=True))
            row = row * scale
            full = work_ref[...]
            col = jnp.sum(jnp.where(lane2 == k, full, 0.0), axis=1, keepdims=True) * scale
            work_ref[...] = full - jnp.where(row1 > k, col, 0.0) * row
            work_ref[pl.ds(k, 1), :] = row

        w_ref[...] = work_ref[:, n:]


def pair(a, b):
    return a * (a + 1) // 2 + b


def chain_kernel(k_ref, out_ref, k_s, w_s, low_s, work_s):
    for i in range(k_ref.shape[0]):
        k_s[i] = k_ref[i]
    for s in range(PANELS):
        invert_block(k_s.at[pair(s, s)], w_s.at[s], work_s)
        w = w_s[s]
        for k in range(s):
            out_ref[pair(s, k)] = dot6(w, low_s[pair(s, k)])
        out_ref[pair(s, s)] = w
        for a in range(s + 1, PANELS):
            low_s[pair(a, s)] = dot6(k_s[pair(a, s)], w, 1)
        for a in range(s + 1, PANELS):
            for b in range(s + 1, a + 1):
                k_s[pair(a, b)] = k_s[pair(a, b)] - dot6(low_s[pair(a, s)], low_s[pair(b, s)], 1)


def chain(corner):
    count, n, _ = corner.shape
    return pl.pallas_call(
        chain_kernel,
        out_shape=jax.ShapeDtypeStruct(corner.shape, jnp.float32),
        in_specs=[pl.BlockSpec(memory_space=pltpu.VMEM)],
        out_specs=pl.BlockSpec(memory_space=pltpu.VMEM),
        scratch_shapes=[pltpu.VMEM((count, n, n), jnp.float32), pltpu.VMEM((PANELS, n, n), jnp.float32),
                        pltpu.VMEM((count, n, n), jnp.float32), pltpu.VMEM((n, 2 * n), jnp.float32)],
        interpret=INTERPRET,
    )(corner)


def spec(space=pltpu.VMEM):
    return pl.BlockSpec(memory_space=space)


def f32(*shape):
    return jax.ShapeDtypeStruct(shape, jnp.float32)


def bf16(*shape):
    return jax.ShapeDtypeStruct(shape, jnp.bfloat16)


def gather_kernel(rows, cols, info, trailing, corner_keep, corner_give, *refs):
    keeps, (gives, sem) = refs[:PANELS], refs[PANELS:]
    my_row, my_col = info[PANELS], info[PANELS + 1]
    half = NB // 2
    count = trailing.shape[1] // NB // 2
    stream = info[PANELS + 3]

    def copy(row, col, out):
        source = trailing.at[
            pl.ds(pl.multiple_of(row, half), out.shape[0]), pl.ds(pl.multiple_of(col, NB), NB)
        ]
        return pltpu.make_async_copy(source, out, sem)

    plans = []
    for a in range(PANELS):
        for b in range(a + 1):
            n = pair(a, b)
            owner = (lax.rem(info[a], rows) == my_row) & (lax.rem(info[b], cols) == my_col)
            per = PANELS * (PANELS + 1) // 4
            place = (n // per == stream, n % per)
            row, col = lax.div(info[a], rows) * NB, lax.div(info[b], cols) * NB
            for keep in (True, False):
                out = corner_keep if keep else corner_give
                jobs = [(row + h * half, col, out.at[2 * place[1] + h]) for h in range(2)]
                plans.append((place[0] == keep, owner, jobs))
    for s in range(PANELS):
        owner = lax.rem(info[s], rows) == my_row
        row = lax.div(info[s], rows) * NB
        jobs = []
        for j in range(count):
            jobs.append((row, (2 * j + stream) * NB, keeps[s].at[j]))
            jobs.append((row, (2 * j + 1 - stream) * NB, gives.at[s * count + j]))
        plans.append((True, owner, jobs))
    for there, owner, jobs in plans:

        @pl.when(there & owner)
        def _():
            for job in jobs:
                copy(*job).start()

        @pl.when(there & jnp.logical_not(owner))
        def _():
            for _, _, out in jobs:
                out[...] = jnp.zeros_like(out)

    for there, owner, jobs in plans:

        @pl.when(there & owner)
        def _():
            for job in jobs:
                copy(*job).wait()


def gather(info, trailing, rows, cols):
    count = trailing.shape[1] // NB // 2
    part = f32(PANELS * (PANELS + 1) // 2, NB // 2, NB)
    shapes = [part, part] + [f32(count, NB, NB)] * PANELS
    shapes.append(f32(PANELS * count, NB, NB))
    return pl.pallas_call(
        lambda *refs: gather_kernel(rows, cols, *refs),
        out_shape=shapes,
        in_specs=[spec(pltpu.SMEM), spec(pl.ANY)],
        out_specs=[spec()] * len(shapes),
        scratch_shapes=[pltpu.SemaphoreType.DMA],
        interpret=INTERPRET,
        cost_estimate=pl.CostEstimate(flops=0, bytes_accessed=16 << 20, transcendentals=0),
    )(info, trailing)


def halves(x):
    high = x.astype(jnp.bfloat16)
    return high, (x - high.astype(jnp.float32)).astype(jnp.bfloat16)


def is_used(info, block, step):
    used = False
    for k in range(step):
        used = used | (block == info[k])
    return used


def params():
    return pltpu.CompilerParams(vmem_limit_bytes=VMEM_LIMIT)


def cost(flops, mib):
    return pl.CostEstimate(flops=flops, bytes_accessed=mib << 20, transcendentals=0)


def block_of(name):
    return pl.BlockSpec((1, NB, NB), lambda i: (pair(*name), 0, 0))


def col_kernel(first, cols, info, *refs):
    width = (PANELS - 1 if first == 0 else PANELS) - first
    raw, refs = refs[:width], refs[width:]
    solved, refs = (refs[:-3], refs[-3:]) if first == 0 else (refs[:1], refs[1:])
    block = (2 * pl.program_id(0) + info[PANELS + 3]) * cols + info[PANELS + 1]
    if first:
        rest, out = refs
        fac = dot6(solved[0][0], raw[0][0]) - rest[0]
        out[0, 0] = jnp.where(is_used(info, block, first), 0.0, fac)
        return
    out, rest, left = refs

    @pl.when(pl.program_id(0) == 0)
    def _():
        for n, ref in enumerate(solved):
            left[n] = left6(ref[0])

    facs = []
    for s in range(width):
        fac = bdot(left[pair(s, s)], right6(raw[s][0]))
        for k in range(s):
            fac = fac - bdot(left[pair(s, k)], facs[k])
        fac = jnp.where(is_used(info, block, s), 0.0, fac)
        facs.append(right6(fac))
        out[s, 0] = fac
    total = None
    for k in range(width):
        term = bdot(left[pair(width, k)], facs[k])
        total = term if total is None else total + term
    rest[0] = total


def col_factor(first, cols, info, raw, solved, rest):
    count = raw[0].shape[0]
    width = len(raw)
    one = pl.BlockSpec((1, NB, NB), lambda i: (i, 0, 0))
    outs = [f32(width, count, NB, NB)]
    specs = [pl.BlockSpec((width, 1, NB, NB), lambda i: (0, i, 0, 0))]
    scratch = []
    if first:
        names = [(first, first)]
    else:
        names = [(a, b) for a in range(PANELS) for b in range(a + 1)][:-1]
        outs.append(f32(count, NB, NB))
        specs.append(one)
        scratch.append(pltpu.VMEM((len(names), NB, 6 * NB), jnp.bfloat16))
    return pl.pallas_call(
        lambda *refs: col_kernel(first, cols, *refs),
        grid=(count,),
        out_shape=outs,
        in_specs=[spec(pltpu.SMEM)]
        + [one] * width
        + [block_of(n) for n in names]
        + [one] * len(rest),
        out_specs=specs,
        scratch_shapes=scratch,
        compiler_params=params(),
        interpret=INTERPRET,
        cost_estimate=cost(12 * len(names) * count * NB**3, 8),
    )(info, *raw, *[solved] * len(names), *rest)


def fetch(info, sources, raw, sem):
    for which, source in enumerate(sources):

        @pl.when(info[PANELS + 2] == which)
        def _():
            copy = pltpu.make_async_copy(source, raw, sem)
            copy.start()
            copy.wait()


def row_kernel(s, rows, count, info, *refs):
    sources, refs = refs[:count], refs[count:]
    last = PANELS - 1
    total = (s + 1) + (PANELS - 1 if s == last - 1 else 0)
    solved, refs = refs[:total], refs[total:]
    before, refs = refs[:s], refs[s:]
    out, parts, raw, sem = refs[0], refs[1], refs[-2], refs[-1]
    step = pl.program_id(0)

    @pl.when(step == 0)
    def _():
        fetch(info, sources, raw, sem)

    fac = dot6(raw[step].T, solved[s][0], 1)
    facs = [ref[...] for ref in before]
    for k in range(s):
        fac = fac - dot6(facs[k], solved[k][0], 1)
    fac = jnp.where(is_used(info, step * rows + info[PANELS], s), 0.0, fac)
    out[...] = fac
    for i, part in enumerate(halves(fac)):
        parts[:, i * NB : (i + 1) * NB] = part
    if s == last - 1:
        facs.append(fac)
        rest = None
        for k in range(last):
            term = dot6(facs[k], solved[s + 1 + k][0], 1)
            rest = term if rest is None else rest + term
        refs[2][...] = rest


def row_factor(s, rows, info, sources, solved, before):
    raw = sources[0].shape
    count = raw[0]
    height = count * NB
    names = [(s, k) for k in range(s + 1)]
    shapes = [f32(height, PANELS * NB), bf16(height, 2 * NB)]
    specs = [
        pl.BlockSpec((NB, NB), lambda i: (i, s)),
        pl.BlockSpec((NB, 2 * NB), lambda i: (i, 0)),
    ]
    if s == PANELS - 2:
        names += [(PANELS - 1, k) for k in range(PANELS - 1)]
        shapes.append(f32(height, NB))
        specs.append(pl.BlockSpec((NB, NB), lambda i: (i, 0)))

    def column(k):
        return pl.BlockSpec((NB, NB), lambda i: (i, k))

    return pl.pallas_call(
        lambda *refs: row_kernel(s, rows, len(sources), *refs),
        grid=(count,),
        out_shape=shapes,
        in_specs=[spec(pltpu.SMEM)]
        + [spec(pltpu.HBM)] * len(sources)
        + [block_of(n) for n in names]
        + [column(k) for k in range(s)],
        out_specs=specs,
        scratch_shapes=[pltpu.VMEM(raw, jnp.float32), pltpu.SemaphoreType.DMA],
        input_output_aliases={1 + len(sources) + len(names): 0} if s else {},
        compiler_params=params(),
        interpret=INTERPRET,
        cost_estimate=cost(12 * len(names) * count * NB**3, 8),
    )(info, *sources, *[solved] * len(names), *before * s)


def set_left(left, parts):
    for k, part in enumerate(parts):
        for i, at in enumerate((0, 1, 0)):
            to = (3 * k + i) * NB
            left[:, to : to + NB] = part[:, at * NB : (at + 1) * NB]


def set_right(right, own, other):
    count = pl.num_programs(0) // 2
    step = pl.program_id(0)
    for there, fac in ((step < count, own), (step >= count, other)):

        @pl.when(there)
        def _():
            for k in range(fac.shape[0]):
                high, low = halves(fac[k, 0])
                for i, part in enumerate((low, high, high)):
                    to = (3 * k + i) * NB
                    right[to : to + NB] = part


def column_at(count, step, info):
    stream = info[PANELS + 3]
    mine = step < count
    return 2 * jnp.where(mine, step, step - count) + jnp.where(mine, stream, 1 - stream)


def update_specs(height, width, panels):
    count = width // NB // 2
    strip = pl.BlockSpec((height, NB), lambda i, info: (0, column_at(count, i, info)))
    shape = (panels, 1, NB, NB)
    own = pl.BlockSpec(shape, lambda i, info: (0, jnp.minimum(i, count - 1), 0, 0))
    other = pl.BlockSpec(shape, lambda i, info: (0, jnp.maximum(i - count, 0), 0, 0))
    return strip, own, other


def early_kernel(info, current, own, other, *refs):
    rparts, out, left, right = refs[:-3], *refs[-3:]

    @pl.when(pl.program_id(0) == 0)
    def _():
        set_left(left, rparts)

    set_right(right, own, other)
    product = jnp.dot(left[...], right[...], preferred_element_type=jnp.float32)
    out[...] = current[...] - product


def early_update(info, current, own, other, rparts):
    height, width = current.shape
    panels = len(rparts)
    strip, mine, theirs = update_specs(height, width, panels)
    return pl.pallas_call(
        early_kernel,
        grid_spec=pltpu.PrefetchScalarGridSpec(
            num_scalar_prefetch=1,
            grid=(width // NB,),
            in_specs=[strip, mine, theirs] + [spec()] * panels,
            out_specs=strip,
            scratch_shapes=[
                pltpu.VMEM((height, 3 * panels * NB), jnp.bfloat16),
                pltpu.VMEM((3 * panels * NB, NB), jnp.bfloat16),
            ],
        ),
        out_shape=f32(height, width),
        compiler_params=params(),
        interpret=INTERPRET,
        cost_estimate=cost(12 * height * width * NB, 24),
    )(info, current, own, other, *rparts)


def last_kernel(rows, cols, count, info, *refs):
    sources, refs = refs[:count], refs[count:]
    current, own, other, w, row_rest, _, out, fout = refs[:8]
    raw, fac_s, left, right, sem, out_sem = refs[8:]
    last = PANELS - 1
    step = pl.program_id(0)
    blk_rows = raw.shape[0]
    write = pltpu.make_async_copy(fac_s, fout.at[:, pl.ds(last * NB, NB)], out_sem)

    @pl.when(step == 0)
    def _():
        fetch(info, sources, raw, sem)
        split = right6(w[0], 1)
        for i in range(blk_rows):
            at = slice(i * NB, (i + 1) * NB)
            fac = bdot(left6(raw[i].T), split, 1) - row_rest[at]
            fac = jnp.where(is_used(info, i * rows + info[PANELS], last), 0.0, fac)
            fac_s[at] = fac
            high, low = halves(fac)
            for k, part in enumerate((high, low, high)):
                left[at, k * NB : (k + 1) * NB] = part

    @pl.when(step == 1)
    def _():
        write.start()

    set_right(right, own, other)
    product = jnp.dot(left[...], right[...], preferred_element_type=jnp.float32)
    value = current[...] - product
    block = column_at(pl.num_programs(0) // 2, step, info) * cols + info[PANELS + 1]
    dead = is_used(info, block, PANELS)
    for i in range(blk_rows):
        used = dead | is_used(info, i * rows + info[PANELS], PANELS)
        at = slice(i * NB, (i + 1) * NB)
        out[at, :] = jnp.where(used, 0.0, value[at])

    @pl.when(step == pl.num_programs(0) - 1)
    def _():
        write.wait()


def last_update(rows, cols, info, sources, current, own, other, solved, row_rest, out):
    height, width = current.shape
    strip, mine, theirs = update_specs(height, width, 1)
    last = PANELS - 1
    count = len(sources)
    w = pl.BlockSpec((1, NB, NB), lambda i, info: (pair(last, last), 0, 0))
    return pl.pallas_call(
        lambda *refs: last_kernel(rows, cols, count, *refs),
        grid_spec=pltpu.PrefetchScalarGridSpec(
            num_scalar_prefetch=1,
            grid=(width // NB,),
            in_specs=[spec(pltpu.HBM)] * count
            + [strip, mine, theirs, w, spec(), spec(pl.ANY)],
            out_specs=[strip, spec(pl.ANY)],
            scratch_shapes=[
                pltpu.VMEM(sources[0].shape, jnp.float32),
                pltpu.VMEM((height, NB), jnp.float32),
                pltpu.VMEM((height, 3 * NB), jnp.bfloat16),
                pltpu.VMEM((3 * NB, NB), jnp.bfloat16),
                pltpu.SemaphoreType.DMA,
                pltpu.SemaphoreType.DMA,
            ],
        ),
        out_shape=[f32(height, width), f32(*out.shape)],
        input_output_aliases={count + 6: 1},
        compiler_params=params(),
        interpret=INTERPRET,
        cost_estimate=cost(6 * height * width * NB, 24),
    )(info, *sources, current, own, other, solved, row_rest, out)


class Net:
    def __init__(self, rows, cols):
        self.rows, self.cols = rows, cols
        self.row_bits = [1 << i for i in range(1, rows.bit_length() - 1)]
        self.col_bits = [1 << i for i in range(cols.bit_length() - 1)]

    def send(self, value, target):
        pairs = []
        for r in range(self.rows):
            for c in range(self.cols):
                to = target(r, c)
                if to is not None:
                    pairs.append((r * self.cols + c, to[0] * self.cols + to[1]))
        return lax.ppermute(value, AXES, pairs)

    def core(self, value):
        return self.send(value, lambda r, c: (r ^ 1, c))

    def step_bit(self, step, core):
        return self.row_bits[(step + core) % len(self.row_bits)]

    def stream(self, r, c):
        return (r + c + r // self.cols) & 1

    def raw_step(self, value, step):
        def target(r, c):
            g = self.stream(r, c)
            to = r ^ self.step_bit(step, g)
            return (to if self.stream(to, c) == g else to ^ 1, c)

        return self.send(value, target)

    def stream_step(self, value, bit):
        def target(r, c):
            to = c ^ bit
            return (r if self.stream(r, to) == self.stream(r, c) else r ^ 1, to)

        return self.send(value, target)

    def col_step(self, value, bit):
        return self.send(value, lambda r, c: (r, c ^ bit))

    def my_bit(self, my_row, stream, step):
        even = (my_row & self.step_bit(step, 0)) != 0
        odd = (my_row & self.step_bit(step, 1)) != 0
        return jnp.where(stream == 0, even, odd).astype(jnp.int32)


def pick(value, index):
    return lax.dynamic_index_in_dim(value, index, 0, keepdims=False)


def spread_corner(net, part, my_row, stream):
    tail = part.shape[1:]
    bits = []
    for step in range(len(net.row_bits)):
        bit = net.my_bit(my_row, stream, step)
        bits.append(bit)
        part = part.reshape((2, -1) + tail)
        part = pick(part, bit) + net.raw_step(pick(part, 1 - bit), step)
    for bit in net.col_bits:
        part = part + net.stream_step(part, bit)
    for step in reversed(range(len(net.row_bits))):
        other = net.raw_step(part, step)
        low = bits[step] == 0
        part = jnp.concatenate([jnp.where(low, part, other), jnp.where(low, other, part)])
    other = net.core(part)
    low = stream == 0
    return jnp.concatenate([jnp.where(low, part, other), jnp.where(low, other, part)])


def spread_rows(net, source, is_source, direct):
    if (net.rows, net.cols) != (8, 4):
        value = jnp.where(is_source, source, 0.0)
        for bit in net.col_bits:
            value = value + net.col_step(value, bit)
        return [value]

    def hop(first, second):
        def target(r, c):
            up = (r // 2) % 2 == 0
            line = c if up else 3 - c
            near = (r % 2 == 0) == up
            to = (first if near else second).get(line)
            if to is None:
                return None
            return (r, to if up else 3 - to)

        return target

    got1 = net.send(source, hop({0: 1}, {1: 2}))
    if direct:
        got2 = net.send(source, hop({0: 2}, {1: 3}))
        got3 = net.send(source, hop({0: 3}, {1: 0}))
        return [source, got1, got2, got3]
    got2 = net.send(got1, hop({1: 2}, {2: 3}))
    third = jnp.where(is_source, source, got2)
    got3 = net.send(third, hop({2: 3}, {1: 0}))
    return [source, got1, got2, got3]


def source_code(net, my_row, my_col):
    if (net.rows, net.cols) != (8, 4):
        return jnp.int32(0)
    up = (my_row & 2) == 0
    line = jnp.where(up, my_col, 3 - my_col)
    near = ((my_row & 1) == 0) == up
    return jnp.where(near, line, (line + 3) & 3)


def run(panel, trailing):
    rows = lax.axis_size("row")
    cols = lax.axis_size("col")
    my_row = lax.axis_index("row")
    my_col = lax.axis_index("col")
    net = Net(rows, cols)
    loc_cols = trailing.shape[1]
    count = loc_cols // NB // 2
    ratio = rows // cols
    group = lax.div(my_row, cols)
    stream = (my_row + my_col + group) & 1
    code = source_code(net, my_row, my_col)
    extra = jnp.stack([my_row, my_col, code, stream])
    info = jnp.concatenate([panel[:PANELS], extra])
    is_source = my_col == lax.rem(my_row, cols)

    corner, corner_give, *keeps, gives = gather(info, trailing, rows, cols)
    got = net.core(gives).reshape(PANELS, count, NB, NB)
    corner = corner + net.core(corner_give)
    corner = spread_corner(net, corner.reshape(rows, -1, NB), my_row, stream)
    solved = chain(corner.reshape(-1, NB, NB))

    raws, sources = [], []
    mixed = []
    for s in range(PANELS):
        kept = keeps[s]
        if mixed:
            kept, _ = lax.optimization_barrier((kept, mixed[0]))
        mixed.append(kept + got[s])
    for s in range(PANELS):
        raw = mixed[s]
        for step in range(len(net.row_bits)):
            raw = raw + net.raw_step(raw, step)
        raws.append(raw)
        own = raw
        if ratio != 2:
            other = net.core(raw)
            even = jnp.where(stream == 0, raw, other)
            odd = jnp.where(stream == 0, other, raw)
            own = jnp.stack([even, odd], axis=1).reshape(-1, ratio, NB, NB)
            own = lax.dynamic_index_in_dim(own, group, 1, keepdims=False)
        sources.append(spread_rows(net, own, is_source, s == PANELS - 1))
    last = PANELS - 1
    early, col_rest = col_factor(0, cols, info, raws[:last], solved, [])
    early_other = net.core(early)
    (late,) = col_factor(last, cols, info, raws[last:], solved, [col_rest])
    late_other = net.core(late)
    out, rparts = (), []
    for s in range(last):
        out, *got = row_factor(s, rows, info, sources[s], solved, [out])
        rparts.append(got[0])
    current = early_update(info, trailing, early, early_other, rparts)
    current, out = last_update(
        rows, cols, info, sources[last], current, late, late_other, solved, got[1], out
    )
    return (out, current)


def solution(mesh):
    in_specs = (P(), P("row", "col"))
    out_specs = (P("row", None), P("row", "col"))
    return jax.shard_map(run, mesh=mesh, in_specs=in_specs, out_specs=out_specs, check_vma=False)
```

```python
import jax
import jax.numpy as jnp
from jax import lax
from jax.experimental import pallas as pl
from jax.experimental.pallas import tpu as pltpu
from jax.sharding import PartitionSpec as P


NB = 256
PANELS = 3
AXES = ("row", "col")
INTERPRET = False
VMEM_LIMIT = 14 << 20


def thirds(x):
    high = x.astype(jnp.bfloat16)
    rest = x - high.astype(jnp.float32)
    mid = rest.astype(jnp.bfloat16)
    return high, mid, (rest - mid.astype(jnp.float32)).astype(jnp.bfloat16)


def left6(a):
    high, mid, low = thirds(a)
    return jnp.concatenate([mid, low, high, mid, high, high], axis=1)


def right6(b, axis=0):
    high, mid, low = thirds(b)
    return jnp.concatenate([mid, high, low, high, mid, high], axis=axis)


def bdot(left, right, axis=0):
    return lax.dot_general(
        left, right, (((1,), (axis,)), ((), ())), preferred_element_type=jnp.float32
    )


def dot6(a, b, axis=0):
    return bdot(left6(a), right6(b, axis), axis)


def iotas(shape):
    return (lax.broadcasted_iota(jnp.int32, shape, 0), lax.broadcasted_iota(jnp.int32, shape, 1))


def invert_block(d_ref, w_ref, work_ref):
    n = d_ref.shape[0]
    ii, jj = iotas((n, n))
    eye = ii == jj
    d = d_ref[...]
    diag = jnp.where(eye, d, 0.0)
    by_col = lax.rsqrt(jnp.sum(diag, axis=0, keepdims=True))
    by_row = lax.rsqrt(jnp.sum(diag, axis=1, keepdims=True))

    def half(r):
        return jnp.where(ii > jj, r, jnp.where(eye, 0.5 * r, 0.0))

    res = jnp.where(eye, 0.0, d * by_row * by_col)
    w_ref[...] = jnp.where(eye, by_row, 0.0) - half(res) * by_col

    def cond(carry):
        count, size = carry
        return (count < 12) & (size > 1e-7)

    def body(carry):
        count, _ = carry
        w = w_ref[...]
        s = dot6(dot6(w, d_ref[...]), w, 1)
        res = jnp.where(eye, s - 1.0, s)
        w_ref[...] = w - dot6(half(res), w)
        return count + 1, jnp.sum(res * res)

    _, size = lax.while_loop(cond, body, (jnp.int32(0), jnp.float32(1.0)))
    low_diag = jnp.min(jnp.where(eye, w_ref[...], 1.0))

    @pl.when(jnp.logical_not((size <= 1e-7) & (low_diag > 0.0)))
    def _():
        work_ref[:, :n] = d_ref[...]
        work_ref[:, n:] = jnp.where(eye, 1.0, 0.0)
        _, lane2 = iotas((n, 2 * n))
        row1, _ = iotas((n, 1))
        lane1 = lax.broadcasted_iota(jnp.int32, (1, 2 * n), 1)

        @pl.loop(0, n)
        def _(k):
            row = work_ref[pl.ds(k, 1), :]
            scale = lax.rsqrt(jnp.sum(jnp.where(lane1 == k, row, 0.0), axis=1, keepdims=True))
            row = row * scale
            full = work_ref[...]
            col = jnp.sum(jnp.where(lane2 == k, full, 0.0), axis=1, keepdims=True) * scale
            work_ref[...] = full - jnp.where(row1 > k, col, 0.0) * row
            work_ref[pl.ds(k, 1), :] = row

        w_ref[...] = work_ref[:, n:]


def pair(a, b):
    return a * (a + 1) // 2 + b


def chain_kernel(k_ref, out_ref, k_s, w_s, low_s, work_s):
    for i in range(k_ref.shape[0]):
        k_s[i] = k_ref[i]
    for s in range(PANELS):
        invert_block(k_s.at[pair(s, s)], w_s.at[s], work_s)
        w = w_s[s]
        for k in range(s):
            out_ref[pair(s, k)] = dot6(w, low_s[pair(s, k)])
        out_ref[pair(s, s)] = w
        for a in range(s + 1, PANELS):
            low_s[pair(a, s)] = dot6(k_s[pair(a, s)], w, 1)
        for a in range(s + 1, PANELS):
            for b in range(s + 1, a + 1):
                k_s[pair(a, b)] = k_s[pair(a, b)] - dot6(low_s[pair(a, s)], low_s[pair(b, s)], 1)


def chain(corner):
    count, n, _ = corner.shape
    return pl.pallas_call(
        chain_kernel,
        out_shape=jax.ShapeDtypeStruct(corner.shape, jnp.float32),
        in_specs=[pl.BlockSpec(memory_space=pltpu.VMEM)],
        out_specs=pl.BlockSpec(memory_space=pltpu.VMEM),
        scratch_shapes=[pltpu.VMEM((count, n, n), jnp.float32), pltpu.VMEM((PANELS, n, n), jnp.float32),
                        pltpu.VMEM((count, n, n), jnp.float32), pltpu.VMEM((n, 2 * n), jnp.float32)],
        interpret=INTERPRET,
    )(corner)


def spec(space=pltpu.VMEM):
    return pl.BlockSpec(memory_space=space)


def f32(*shape):
    return jax.ShapeDtypeStruct(shape, jnp.float32)


def bf16(*shape):
    return jax.ShapeDtypeStruct(shape, jnp.bfloat16)


def gather_kernel(rows, cols, info, trailing, corner_keep, corner_give, *refs):
    keeps, (gives, sem) = refs[:PANELS], refs[PANELS:]
    my_row, my_col = info[PANELS], info[PANELS + 1]
    half = NB // 2
    count = trailing.shape[1] // NB // 2
    stream = info[PANELS + 3]

    def copy(row, col, out):
        source = trailing.at[
            pl.ds(pl.multiple_of(row, half), out.shape[0]), pl.ds(pl.multiple_of(col, NB), NB)
        ]
        return pltpu.make_async_copy(source, out, sem)

    plans = []
    for a in range(PANELS):
        for b in range(a + 1):
            n = pair(a, b)
            owner = (lax.rem(info[a], rows) == my_row) & (lax.rem(info[b], cols) == my_col)
            per = PANELS * (PANELS + 1) // 4
            place = (n // per == stream, n % per)
            row, col = lax.div(info[a], rows) * NB, lax.div(info[b], cols) * NB
            for keep in (True, False):
                out = corner_keep if keep else corner_give
                jobs = [(row + h * half, col, out.at[2 * place[1] + h]) for h in range(2)]
                plans.append((place[0] == keep, owner, jobs))
    for s in range(PANELS):
        owner = lax.rem(info[s], rows) == my_row
        row = lax.div(info[s], rows) * NB
        jobs = []
        for j in range(count):
            jobs.append((row, (2 * j + stream) * NB, keeps[s].at[j]))
            jobs.append((row, (2 * j + 1 - stream) * NB, gives.at[s * count + j]))
        plans.append((True, owner, jobs))
    for there, owner, jobs in plans:

        @pl.when(there & owner)
        def _():
            for job in jobs:
                copy(*job).start()

        @pl.when(there & jnp.logical_not(owner))
        def _():
            for _, _, out in jobs:
                out[...] = jnp.zeros_like(out)

    for there, owner, jobs in plans:

        @pl.when(there & owner)
        def _():
            for job in jobs:
                copy(*job).wait()


def gather(info, trailing, rows, cols):
    count = trailing.shape[1] // NB // 2
    part = f32(PANELS * (PANELS + 1) // 2, NB // 2, NB)
    shapes = [part, part] + [f32(count, NB, NB)] * PANELS
    shapes.append(f32(PANELS * count, NB, NB))
    return pl.pallas_call(
        lambda *refs: gather_kernel(rows, cols, *refs),
        out_shape=shapes,
        in_specs=[spec(pltpu.SMEM), spec(pl.ANY)],
        out_specs=[spec()] * len(shapes),
        scratch_shapes=[pltpu.SemaphoreType.DMA],
        interpret=INTERPRET,
        cost_estimate=pl.CostEstimate(flops=0, bytes_accessed=16 << 20, transcendentals=0),
    )(info, trailing)


def halves(x):
    high = x.astype(jnp.bfloat16)
    return high, (x - high.astype(jnp.float32)).astype(jnp.bfloat16)


def is_used(info, block, step):
    used = False
    for k in range(step):
        used = used | (block == info[k])
    return used


def params():
    return pltpu.CompilerParams(vmem_limit_bytes=VMEM_LIMIT)


def cost(flops, mib):
    return pl.CostEstimate(flops=flops, bytes_accessed=mib << 20, transcendentals=0)


def block_of(name):
    return pl.BlockSpec((1, NB, NB), lambda i: (pair(*name), 0, 0))


def col_kernel(first, cols, info, *refs):
    width = (PANELS - 1 if first == 0 else PANELS) - first
    raw, refs = refs[:width], refs[width:]
    solved, refs = (refs[:-3], refs[-3:]) if first == 0 else (refs[:1], refs[1:])
    block = (2 * pl.program_id(0) + info[PANELS + 3]) * cols + info[PANELS + 1]
    if first:
        rest, out = refs
        fac = dot6(solved[0][0], raw[0][0]) - rest[0]
        out[0, 0] = jnp.where(is_used(info, block, first), 0.0, fac)
        return
    out, rest, left = refs

    @pl.when(pl.program_id(0) == 0)
    def _():
        for n, ref in enumerate(solved):
            left[n] = left6(ref[0])

    facs = []
    for s in range(width):
        fac = bdot(left[pair(s, s)], right6(raw[s][0]))
        for k in range(s):
            fac = fac - bdot(left[pair(s, k)], facs[k])
        fac = jnp.where(is_used(info, block, s), 0.0, fac)
        facs.append(right6(fac))
        out[s, 0] = fac
    total = None
    for k in range(width):
        term = bdot(left[pair(width, k)], facs[k])
        total = term if total is None else total + term
    rest[0] = total


def col_factor(first, cols, info, raw, solved, rest):
    count = raw[0].shape[0]
    width = len(raw)
    one = pl.BlockSpec((1, NB, NB), lambda i: (i, 0, 0))
    outs = [f32(width, count, NB, NB)]
    specs = [pl.BlockSpec((width, 1, NB, NB), lambda i: (0, i, 0, 0))]
    scratch = []
    if first:
        names = [(first, first)]
    else:
        names = [(a, b) for a in range(PANELS) for b in range(a + 1)][:-1]
        outs.append(f32(count, NB, NB))
        specs.append(one)
        scratch.append(pltpu.VMEM((len(names), NB, 6 * NB), jnp.bfloat16))
    return pl.pallas_call(
        lambda *refs: col_kernel(first, cols, *refs),
        grid=(count,),
        out_shape=outs,
        in_specs=[spec(pltpu.SMEM)]
        + [one] * width
        + [block_of(n) for n in names]
        + [one] * len(rest),
        out_specs=specs,
        scratch_shapes=scratch,
        compiler_params=params(),
        interpret=INTERPRET,
        cost_estimate=cost(12 * len(names) * count * NB**3, 8),
    )(info, *raw, *[solved] * len(names), *rest)


def fetch(info, sources, raw, sem):
    for which, source in enumerate(sources):

        @pl.when(info[PANELS + 2] == which)
        def _():
            copy = pltpu.make_async_copy(source, raw, sem)
            copy.start()
            copy.wait()


def row_kernel(s, rows, count, info, *refs):
    sources, refs = refs[:count], refs[count:]
    last = PANELS - 1
    total = (s + 1) + (PANELS - 1 if s == last - 1 else 0)
    solved, refs = refs[:total], refs[total:]
    before, refs = refs[:s], refs[s:]
    out, parts, raw, sem = refs[0], refs[1], refs[-2], refs[-1]
    step = pl.program_id(0)

    @pl.when(step == 0)
    def _():
        fetch(info, sources, raw, sem)

    fac = dot6(raw[step].T, solved[s][0], 1)
    facs = [ref[...] for ref in before]
    for k in range(s):
        fac = fac - dot6(facs[k], solved[k][0], 1)
    fac = jnp.where(is_used(info, step * rows + info[PANELS], s), 0.0, fac)
    out[...] = fac
    for i, part in enumerate(halves(fac)):
        parts[:, i * NB : (i + 1) * NB] = part
    if s == last - 1:
        facs.append(fac)
        rest = None
        for k in range(last):
            term = dot6(facs[k], solved[s + 1 + k][0], 1)
            rest = term if rest is None else rest + term
        refs[2][...] = rest


def row_factor(s, rows, info, sources, solved, before):
    raw = sources[0].shape
    count = raw[0]
    height = count * NB
    names = [(s, k) for k in range(s + 1)]
    shapes = [f32(height, PANELS * NB), bf16(height, 2 * NB)]
    specs = [
        pl.BlockSpec((NB, NB), lambda i: (i, s)),
        pl.BlockSpec((NB, 2 * NB), lambda i: (i, 0)),
    ]
    if s == PANELS - 2:
        names += [(PANELS - 1, k) for k in range(PANELS - 1)]
        shapes.append(f32(height, NB))
        specs.append(pl.BlockSpec((NB, NB), lambda i: (i, 0)))

    def column(k):
        return pl.BlockSpec((NB, NB), lambda i: (i, k))

    return pl.pallas_call(
        lambda *refs: row_kernel(s, rows, len(sources), *refs),
        grid=(count,),
        out_shape=shapes,
        in_specs=[spec(pltpu.SMEM)]
        + [spec(pltpu.HBM)] * len(sources)
        + [block_of(n) for n in names]
        + [column(k) for k in range(s)],
        out_specs=specs,
        scratch_shapes=[pltpu.VMEM(raw, jnp.float32), pltpu.SemaphoreType.DMA],
        input_output_aliases={1 + len(sources) + len(names): 0} if s else {},
        compiler_params=params(),
        interpret=INTERPRET,
        cost_estimate=cost(12 * len(names) * count * NB**3, 8),
    )(info, *sources, *[solved] * len(names), *before * s)


def set_left(left, parts):
    for k, part in enumerate(parts):
        for i, at in enumerate((0, 1, 0)):
            to = (3 * k + i) * NB
            left[:, to : to + NB] = part[:, at * NB : (at + 1) * NB]


def set_right(right, own, other):
    count = pl.num_programs(0) // 2
    step = pl.program_id(0)
    for there, fac in ((step < count, own), (step >= count, other)):

        @pl.when(there)
        def _():
            for k in range(fac.shape[0]):
                high, low = halves(fac[k, 0])
                for i, part in enumerate((low, high, high)):
                    to = (3 * k + i) * NB
                    right[to : to + NB] = part


def column_at(count, step, info):
    stream = info[PANELS + 3]
    mine = step < count
    return 2 * jnp.where(mine, step, step - count) + jnp.where(mine, stream, 1 - stream)


def update_specs(height, width, panels):
    count = width // NB // 2
    strip = pl.BlockSpec((height, NB), lambda i, info: (0, column_at(count, i, info)))
    shape = (panels, 1, NB, NB)
    own = pl.BlockSpec(shape, lambda i, info: (0, jnp.minimum(i, count - 1), 0, 0))
    other = pl.BlockSpec(shape, lambda i, info: (0, jnp.maximum(i - count, 0), 0, 0))
    return strip, own, other


def early_kernel(info, current, own, other, *refs):
    rparts, out, left, right = refs[:-3], *refs[-3:]

    @pl.when(pl.program_id(0) == 0)
    def _():
        set_left(left, rparts)

    set_right(right, own, other)
    product = jnp.dot(left[...], right[...], preferred_element_type=jnp.float32)
    out[...] = current[...] - product


def early_update(info, current, own, other, rparts):
    height, width = current.shape
    panels = len(rparts)
    strip, mine, theirs = update_specs(height, width, panels)
    return pl.pallas_call(
        early_kernel,
        grid_spec=pltpu.PrefetchScalarGridSpec(
            num_scalar_prefetch=1,
            grid=(width // NB,),
            in_specs=[strip, mine, theirs] + [spec()] * panels,
            out_specs=strip,
            scratch_shapes=[
                pltpu.VMEM((height, 3 * panels * NB), jnp.bfloat16),
                pltpu.VMEM((3 * panels * NB, NB), jnp.bfloat16),
            ],
        ),
        out_shape=f32(height, width),
        compiler_params=params(),
        interpret=INTERPRET,
        cost_estimate=cost(12 * height * width * NB, 24),
    )(info, current, own, other, *rparts)


def last_kernel(rows, cols, count, info, *refs):
    sources, refs = refs[:count], refs[count:]
    current, own, other, w, row_rest, _, out, fout = refs[:8]
    raw, fac_s, left, right, sem, out_sem = refs[8:]
    last = PANELS - 1
    step = pl.program_id(0)
    blk_rows = raw.shape[0]
    write = pltpu.make_async_copy(fac_s, fout.at[:, pl.ds(last * NB, NB)], out_sem)

    @pl.when(step == 0)
    def _():
        fetch(info, sources, raw, sem)
        split = right6(w[0], 1)
        for i in range(blk_rows):
            at = slice(i * NB, (i + 1) * NB)
            fac = bdot(left6(raw[i].T), split, 1) - row_rest[at]
            fac = jnp.where(is_used(info, i * rows + info[PANELS], last), 0.0, fac)
            fac_s[at] = fac
            high, low = halves(fac)
            for k, part in enumerate((high, low, high)):
                left[at, k * NB : (k + 1) * NB] = part

    @pl.when(step == 1)
    def _():
        write.start()

    set_right(right, own, other)
    product = jnp.dot(left[...], right[...], preferred_element_type=jnp.float32)
    value = current[...] - product
    block = column_at(pl.num_programs(0) // 2, step, info) * cols + info[PANELS + 1]
    dead = is_used(info, block, PANELS)
    for i in range(blk_rows):
        used = dead | is_used(info, i * rows + info[PANELS], PANELS)
        at = slice(i * NB, (i + 1) * NB)
        out[at, :] = jnp.where(used, 0.0, value[at])

    @pl.when(step == pl.num_programs(0) - 1)
    def _():
        write.wait()


def last_update(rows, cols, info, sources, current, own, other, solved, row_rest, out):
    height, width = current.shape
    strip, mine, theirs = update_specs(height, width, 1)
    last = PANELS - 1
    count = len(sources)
    w = pl.BlockSpec((1, NB, NB), lambda i, info: (pair(last, last), 0, 0))
    return pl.pallas_call(
        lambda *refs: last_kernel(rows, cols, count, *refs),
        grid_spec=pltpu.PrefetchScalarGridSpec(
            num_scalar_prefetch=1,
            grid=(width // NB,),
            in_specs=[spec(pltpu.HBM)] * count
            + [strip, mine, theirs, w, spec(), spec(pltpu.HBM)],
            out_specs=[strip, spec(pltpu.HBM)],
            scratch_shapes=[
                pltpu.VMEM(sources[0].shape, jnp.float32),
                pltpu.VMEM((height, NB), jnp.float32),
                pltpu.VMEM((height, 3 * NB), jnp.bfloat16),
                pltpu.VMEM((3 * NB, NB), jnp.bfloat16),
                pltpu.SemaphoreType.DMA,
                pltpu.SemaphoreType.DMA,
            ],
        ),
        out_shape=[f32(height, width), f32(*out.shape)],
        input_output_aliases={count + 6: 1},
        compiler_params=params(),
        interpret=INTERPRET,
        cost_estimate=cost(6 * height * width * NB, 24),
    )(info, *sources, current, own, other, solved, row_rest, out)


class Net:
    def __init__(self, rows, cols):
        self.rows, self.cols = rows, cols
        self.row_bits = [1 << i for i in range(1, rows.bit_length() - 1)]
        self.col_bits = [1 << i for i in range(cols.bit_length() - 1)]

    def send(self, value, target):
        pairs = []
        for r in range(self.rows):
            for c in range(self.cols):
                to = target(r, c)
                if to is not None:
                    pairs.append((r * self.cols + c, to[0] * self.cols + to[1]))
        return lax.ppermute(value, AXES, pairs)

    def core(self, value):
        return self.send(value, lambda r, c: (r ^ 1, c))

    def step_bit(self, step, core):
        return self.row_bits[(step + core) % len(self.row_bits)]

    def stream(self, r, c):
        return (r + c + r // self.cols) & 1

    def raw_step(self, value, step):
        def target(r, c):
            g = self.stream(r, c)
            to = r ^ self.step_bit(step, g)
            return (to if self.stream(to, c) == g else to ^ 1, c)

        return self.send(value, target)

    def stream_step(self, value, bit):
        def target(r, c):
            to = c ^ bit
            return (r if self.stream(r, to) == self.stream(r, c) else r ^ 1, to)

        return self.send(value, target)

    def col_step(self, value, bit):
        return self.send(value, lambda r, c: (r, c ^ bit))

    def my_bit(self, my_row, stream, step):
        even = (my_row & self.step_bit(step, 0)) != 0
        odd = (my_row & self.step_bit(step, 1)) != 0
        return jnp.where(stream == 0, even, odd).astype(jnp.int32)


def pick(value, index):
    return lax.dynamic_index_in_dim(value, index, 0, keepdims=False)


def spread_corner(net, part, my_row, stream):
    tail = part.shape[1:]
    bits = []
    for step in range(len(net.row_bits)):
        bit = net.my_bit(my_row, stream, step)
        bits.append(bit)
        part = part.reshape((2, -1) + tail)
        part = pick(part, bit) + net.raw_step(pick(part, 1 - bit), step)
    for bit in net.col_bits:
        part = part + net.stream_step(part, bit)
    for step in reversed(range(len(net.row_bits))):
        other = net.raw_step(part, step)
        low = bits[step] == 0
        part = jnp.concatenate([jnp.where(low, part, other), jnp.where(low, other, part)])
    other = net.core(part)
    low = stream == 0
    return jnp.concatenate([jnp.where(low, part, other), jnp.where(low, other, part)])


def spread_rows(net, source, is_source, near):
    if (net.rows, net.cols) != (8, 4):
        value = jnp.where(is_source, source, 0.0)
        for bit in net.col_bits:
            value = value + net.col_step(value, bit)
        return [value]

    def hop(first, second):
        def target(r, c):
            up = (r // 2) % 2 == 0
            line = c if up else 3 - c
            near = (r % 2 == 0) == up
            to = (first if near else second).get(line)
            if to is None:
                return None
            return (r, to if up else 3 - to)

        return target

    got1 = net.send(source, hop({0: 1}, {1: 2}))
    got2 = net.send(source, hop({0: 2}, {1: 0}))
    third = jnp.where(near, got2, got1)
    got3 = net.send(third, hop({2: 3}, {2: 3}))
    return [source, got1, got2, got3]


def source_code(net, my_row, my_col):
    if (net.rows, net.cols) != (8, 4):
        return jnp.int32(0), True
    up = (my_row & 2) == 0
    line = jnp.where(up, my_col, 3 - my_col)
    near = ((my_row & 1) == 0) == up
    far = jnp.where(line == 3, 3, jnp.where(line == 0, 2, line - 1))
    return jnp.where(near, line, far), near


def run(panel, trailing):
    rows = lax.axis_size("row")
    cols = lax.axis_size("col")
    my_row = lax.axis_index("row")
    my_col = lax.axis_index("col")
    net = Net(rows, cols)
    loc_cols = trailing.shape[1]
    count = loc_cols // NB // 2
    ratio = rows // cols
    group = lax.div(my_row, cols)
    stream = (my_row + my_col + group) & 1
    code, near = source_code(net, my_row, my_col)
    extra = jnp.stack([my_row, my_col, code, stream])
    info = jnp.concatenate([panel[:PANELS], extra])
    is_source = my_col == lax.rem(my_row, cols)

    corner, corner_give, *keeps, gives = gather(info, trailing, rows, cols)
    got = net.core(gives).reshape(PANELS, count, NB, NB)
    corner = corner + net.core(corner_give)
    corner = spread_corner(net, corner.reshape(rows, -1, NB), my_row, stream)
    solved = chain(corner.reshape(-1, NB, NB))

    raws, sources = [], []
    mixed = []
    for s in range(PANELS):
        kept = keeps[s]
        if mixed:
            kept, _ = lax.optimization_barrier((kept, mixed[0]))
        mixed.append(kept + got[s])
    for s in range(PANELS):
        raw = mixed[s]
        for step in range(len(net.row_bits)):
            moved = net.raw_step(raw, step)
            raw = raw + moved
        raws.append(raw)
        own = raw
        if ratio != 2:
            other = net.core(raw)
            even = jnp.where(stream == 0, raw, other)
            odd = jnp.where(stream == 0, other, raw)
            own = jnp.stack([even, odd], axis=1).reshape(-1, ratio, NB, NB)
            own = lax.dynamic_index_in_dim(own, group, 1, keepdims=False)
        sources.append(spread_rows(net, own, is_source, near))
    last = PANELS - 1
    early, col_rest = col_factor(0, cols, info, raws[:last], solved, [])
    early_other = net.core(early)
    (late,) = col_factor(last, cols, info, raws[last:], solved, [col_rest])
    late_other = net.core(late)
    out, rparts = (), []
    for s in range(last):
        out, *got = row_factor(s, rows, info, sources[s], solved, [out])
        rparts.append(got[0])
    current = early_update(info, trailing, early, early_other, rparts)
    current, out = last_update(
        rows, cols, info, sources[last], current, late, late_other, solved, got[1], out
    )
    return (out, current)


def solution(mesh):
    in_specs = (P(), P("row", "col"))
    out_specs = (P("row", None), P("row", "col"))
    return jax.shard_map(run, mesh=mesh, in_specs=in_specs, out_specs=out_specs, check_vma=False)
```
